256 devices in a mesh: fsdp: 16 (over x_hi, y, core), ep: 16 (over x_lo, z).
Axes of the slice: x: 4 (x_hi: 2, x_lo: 2; x = x_hi * 2 + x_lo), y: 4, z: 8, core: 2. Of those that a mesh axis runs over, the one named last changes fastest.
Arguments:
- tokens: bfloat16 [65536, 2048], P(('fsdp', 'ep')), may hold values from -6 to 6
- out_grad: bfloat16 [65536, 2048], P(('fsdp', 'ep')), may hold values from -4 to 4
- expert_ids: int32 [65536, 8], P(('fsdp', 'ep')), may hold values from 0 to 127, as said below
- gate_probs: bfloat16 [65536, 8], P(('fsdp', 'ep')), may hold values from 0.19921875 to 1
- w_gate: bfloat16 [2048, 16, 768], P('fsdp', 'ep'), may hold values from -0.125 to 0.125
- w_up: bfloat16 [2048, 16, 768], P('fsdp', 'ep'), may hold values from -0.125 to 0.125
- w_down: bfloat16 [2048, 16, 768], P('fsdp', 'ep'), may hold values from -0.21875 to 0.21875
Outputs:
- in_grad: bfloat16 [65536, 2048], P(('fsdp', 'ep'))
- gate_grad: bfloat16 [65536, 8], P(('fsdp', 'ep'))
- grad_gate: bfloat16 [2048, 16, 768], P('fsdp', 'ep')
- grad_up: bfloat16 [2048, 16, 768], P('fsdp', 'ep')
- grad_down: bfloat16 [2048, 16, 768], P('fsdp', 'ep')
The draws below stay inside these ranges and needn't reach their ends.
Inputs may be any that keep to these rules, and one draw needn't show every extreme that they name: `expert_ids`: each token names 8 different experts. Among the 256 tokens of one device each expert below 16 is named by at most 32 tokens; in each group of devices that share an index of fsdp, one expert below 16 is named by exactly 32 tokens of every device of the group.
All inputs are finite; a program needn't handle non-finite values.
Results may differ from the reference program's by a relative error of at most 0.014.
Values may be sent and summed in bfloat16 or wider, within the bound.
A program may use at most 128 MiB of HBM per device.

```python
import jax
import jax.numpy as jnp
from jax import lax

D = 2048
FF = 768
EXPERTS = 128
TOPK = 8
TOK_DEV = 256
MOST = 32
WIN = 16
TOKENS = 65536
N_FSDP = 16
N_EP = 16


def draw_expert_ids(key, part):
    blocks = TOKENS // TOK_DEV
    per_column = (N_EP + TOPK - 1) // TOPK
    keys = jax.random.split(jax.random.fold_in(key, 7), 5)
    counts = jax.random.randint(keys[0], (blocks, N_EP), 0, MOST)
    hottest = jax.random.randint(keys[1], (blocks // N_EP,), 0, N_EP)
    hot_rows = jnp.repeat(hottest, N_EP)
    counts = jnp.where(jnp.arange(N_EP)[None, :] == hot_rows[:, None], MOST, counts)
    padded = jnp.concatenate([counts, jnp.zeros((blocks, per_column * TOPK - N_EP), jnp.int32)], axis=1)
    padded = padded.reshape(blocks, per_column, TOPK)
    ends = jnp.cumsum(padded, axis=1)
    starts = ends - padded
    scores = jax.random.randint(keys[2], (blocks, TOPK, TOK_DEV), 0, 1 << 20) * TOK_DEV + jnp.arange(TOK_DEV)[None, None, :]
    order = jnp.argsort(scores, axis=-1)
    ranks = jnp.argsort(order, axis=-1)
    inside = (ranks[:, None, :, :] >= starts[:, :, :, None]) & (ranks[:, None, :, :] < ends[:, :, :, None])
    numbers = jnp.arange(per_column)[:, None] * TOPK + jnp.arange(TOPK)[None, :]
    window_ids = jnp.sum(jnp.where(inside, numbers[None, :, :, None] + 1, 0), axis=1) - 1
    window_ids = jnp.swapaxes(window_ids, 1, 2)
    others = EXPERTS - N_EP
    offsets = jax.random.randint(keys[3], (blocks, TOK_DEV, 1), 0, others)
    filler = N_EP + (offsets + jnp.arange(TOPK)[None, None, :]) % others
    columns = jnp.where(window_ids >= 0, window_ids, filler)
    column_scores = jax.random.randint(keys[4], (blocks, TOK_DEV, TOPK), 0, 1 << 20) * TOPK + jnp.arange(TOPK)[None, None, :]
    shuffle = jnp.argsort(column_scores, axis=-1)
    result = jnp.take_along_axis(columns, shuffle, axis=-1)
    return result.reshape(TOKENS, TOPK).astype(jnp.int32)


def shard_levels(own_key, dims, cuts, low, high):
    def one(dim, shards_of):
        draws = jax.random.uniform(jax.random.fold_in(jax.random.fold_in(own_key, 6), dim), (shards_of,), jnp.float32, low / len(cuts), high / len(cuts))
        return jnp.repeat(jnp.exp(draws), dims[dim] // shards_of).reshape((-1,) + (1,) * (len(dims) - dim - 1))

    loudness = one(*cuts[0])
    for cut in cuts[1:]:
        loudness = loudness * one(*cut)
    return loudness


def noise(rng, extent, scale, reach, cuts=(), dtype=jnp.bfloat16):
    drawn = scale * jax.random.normal(rng, extent, jnp.float32)
    if cuts:
        drawn = drawn * shard_levels(rng, extent, cuts, -0.22, 0.18)
    return jnp.clip(drawn, -reach, reach).astype(dtype)


def setup_inputs(seed: int = 0) -> dict:
    arg_keys = jax.random.split(jax.random.key(seed), 8)
    tokens = noise(arg_keys[0], (TOKENS, D), 1.0, 6.0, ((0, 256),))
    out_grad = noise(arg_keys[1], (TOKENS, D), 0.5, 4.0, ((0, 256),))
    expert_ids = draw_expert_ids(jax.random.fold_in(arg_keys[7], 71), 0)
    gate_probs = jnp.clip(0.19921875 + 0.80078125 * jax.random.uniform(arg_keys[3], (TOKENS, TOPK), jnp.float32) ** shard_levels(arg_keys[3], (TOKENS, TOPK), ((0, 256),), -0.2, 0.2), 0.19921875, 1.0).astype(jnp.bfloat16)
    w_gate = noise(arg_keys[4], (D, WIN, FF), D ** -0.5, 0.125, ((0, 16), (1, 16)))
    w_up = noise(arg_keys[5], (D, WIN, FF), D ** -0.5, 0.125, ((0, 16), (1, 16)))
    w_down = noise(arg_keys[6], (D, WIN, FF), FF ** -0.5, 0.21875, ((0, 16), (1, 16)))
    return dict(tokens=tokens, out_grad=out_grad, expert_ids=expert_ids, gate_probs=gate_probs, w_gate=w_gate, w_up=w_up, w_down=w_down)


def expert_math(grad_rows, gate_rows, gate_pre, up_pre, back_proj):
    sigmoid_gate = jax.nn.sigmoid(gate_pre)
    silu_gate = gate_pre * sigmoid_gate
    activated = (silu_gate * up_pre).astype(jnp.bfloat16)
    pick_grad = jnp.sum(activated.astype(jnp.float32) * back_proj, axis=-1).astype(jnp.bfloat16)
    weight_col = gate_rows.astype(jnp.float32)[:, None]
    scaled_back = weight_col * back_proj
    gate_delta = (scaled_back * up_pre * sigmoid_gate * (1.0 + gate_pre * (1.0 - sigmoid_gate))).astype(jnp.bfloat16)
    up_delta = (scaled_back * silu_gate).astype(jnp.bfloat16)
    scaled_grad = (weight_col * grad_rows.astype(jnp.float32)).astype(jnp.bfloat16)
    return activated, pick_grad, gate_delta, up_delta, scaled_grad


def reference(tokens, out_grad, expert_ids, gate_probs, w_gate, w_up, w_down):
    group = N_EP * TOK_DEV
    rows_cap = N_EP * MOST

    def one_group(totals, pieces):
        group_tokens, group_grads, group_ids, group_gates = pieces

        def one_expert(carry, expert):
            in_acc, pick_acc = carry
            matches = group_ids == expert
            chosen = jnp.any(matches, axis=1)
            gate_pick = jnp.sum(jnp.where(matches, group_gates.astype(jnp.float32), 0.0), axis=1)
            count = jnp.sum(chosen.astype(jnp.int32))
            positions = jnp.nonzero(chosen, size=rows_cap, fill_value=0)[0].astype(jnp.int32)
            valid = lax.iota(jnp.int32, rows_cap) < count
            row_tokens = jnp.where(valid[:, None], group_tokens[positions], jnp.zeros((), jnp.bfloat16))
            row_grads = jnp.where(valid[:, None], group_grads[positions], jnp.zeros((), jnp.bfloat16))
            row_gates = jnp.where(valid, gate_pick[positions], 0.0).astype(jnp.bfloat16)
            gate_weight = lax.dynamic_index_in_dim(w_gate, expert, 1, keepdims=False)
            up_weight = lax.dynamic_index_in_dim(w_up, expert, 1, keepdims=False)
            down_weight = lax.dynamic_index_in_dim(w_down, expert, 1, keepdims=False)
            gate_pre = jnp.dot(row_tokens, gate_weight, preferred_element_type=jnp.float32)
            up_pre = jnp.dot(row_tokens, up_weight, preferred_element_type=jnp.float32)
            back_proj = jnp.dot(row_grads, down_weight, preferred_element_type=jnp.float32)
            activated, pick_grad, gate_delta, up_delta, scaled_grad = expert_math(row_grads, row_gates, gate_pre, up_pre, back_proj)
            row_in = (jnp.dot(gate_delta, gate_weight.T, preferred_element_type=jnp.float32)
                      + jnp.dot(up_delta, up_weight.T, preferred_element_type=jnp.float32)).astype(jnp.bfloat16)
            in_part = jax.ops.segment_sum(jnp.where(valid[:, None], row_in.astype(jnp.float32), 0.0), positions, num_segments=group)
            pick_tokens = jax.ops.segment_sum(jnp.where(valid, pick_grad.astype(jnp.float32), 0.0), positions, num_segments=group)
            pick_part = jnp.where(matches, pick_tokens[:, None], 0.0)
            part_gate = jnp.dot(row_tokens.T, gate_delta, preferred_element_type=jnp.float32).astype(jnp.bfloat16)
            part_up = jnp.dot(row_tokens.T, up_delta, preferred_element_type=jnp.float32).astype(jnp.bfloat16)
            part_down = jnp.dot(scaled_grad.T, activated, preferred_element_type=jnp.float32).astype(jnp.bfloat16)
            return (in_acc + in_part, pick_acc + pick_part), (part_gate, part_up, part_down)

        start = (jnp.zeros((group, D), jnp.float32), jnp.zeros((group, TOPK), jnp.float32))
        (in_sum, pick_sum), parts = lax.scan(one_expert, start, lax.iota(jnp.int32, N_EP))
        totals = (totals[0] + parts[0].astype(jnp.float32), totals[1] + parts[1].astype(jnp.float32), totals[2] + parts[2].astype(jnp.float32))
        return totals, (in_sum.astype(jnp.bfloat16), pick_sum.astype(jnp.bfloat16))

    pieces = (tokens.reshape(N_FSDP, group, D), out_grad.reshape(N_FSDP, group, D),
              expert_ids.reshape(N_FSDP, group, TOPK), gate_probs.reshape(N_FSDP, group, TOPK))
    zeros_grad = jnp.zeros((N_EP, D, FF), jnp.float32)
    totals, outputs = lax.scan(one_group, (zeros_grad, zeros_grad, zeros_grad), pieces)
    grad_gate = jnp.transpose(totals[0], (1, 0, 2)).astype(jnp.bfloat16)
    grad_up = jnp.transpose(totals[1], (1, 0, 2)).astype(jnp.bfloat16)
    grad_down = jnp.transpose(totals[2], (1, 0, 2)).astype(jnp.bfloat16)
    return outputs[0].reshape(TOKENS, D), outputs[1].reshape(TOKENS, TOPK), grad_gate, grad_up, grad_down
```

```python
import jax
import jax.numpy as jnp
from jax import lax
from jax.experimental import pallas as pl
from jax.experimental.pallas import tpu as pltpu
from jax.sharding import PartitionSpec as P

MESH = pl.DeviceIdType.MESH
BF = jnp.bfloat16
F32 = jnp.float32

MOST = 32
D = 2048
FF = 768
TOK = 256
N_EP = 16
N_Z = 8
ROWS = N_EP * MOST
SHARD = 128
CW = D + 128

OFFS = (
    (0, 0), (1, 0), (0, 1), (0, 7),
    (1, 1), (1, 7), (0, 2), (0, 6),
    (1, 2), (1, 6), (0, 3), (0, 5),
    (1, 3), (1, 5), (0, 4), (1, 4),
)
BLOCKS = ((0, 8), (8, 8))
CHIPS = ((1, 2), (1, 1), (1, 3), (1, 0), (0, 2), (0, 1), (0, 3), (0, 0))


def dot(a, b):
    return jnp.dot(a, b, preferred_element_type=F32)


def kernel(
    tok, og, ids_t, gp_t, ids, gp, wg, wu, wd,
    in_grad, gate_grad, gg, gu, gd,
    w, snd, rcv, xt, qt, dl, hh, cs, cr, tb, sb, ry, xs, rx, pm, ptm, gc,
    w_ss, w_rs, a_ss, a_rs, c_ss, c_rs, s_ss, s_rs, y_ss, y_rs, x_ss, x_rs,
):
    f = lax.axis_index("fsdp")
    e = lax.axis_index("ep")
    xh, y, c = f // 8, (f // 2) % 4, f % 2
    xl, z = e // N_Z, e % N_Z
    sends = []

    def fdev(dx, dy, dc):
        return ((((xh + dx) % 2) * 4 + (y + dy) % 4) * 2 + (c + dc) % 2, e)

    def owner(i, sign):
        dx, dz = OFFS[i]
        return ((xl + dx) % 2) * N_Z + (z + N_Z + sign * dz) % N_Z

    def copy(src, dst, ss, rs, dev):
        return pltpu.make_async_remote_copy(
            src_ref=src, dst_ref=dst, send_sem=ss, recv_sem=rs,
            device_id=dev, device_id_type=MESH,
        )

    def send(*args):
        cp = copy(*args)
        cp.start()
        sends.append(cp)

    def wrows(fs):
        return w.at[pl.ds(pl.multiple_of(fs * SHARD, SHARD), SHARD), :]

    barrier = pltpu.get_barrier_semaphore()
    peers = [(f, owner(i, 1)) for i in range(1, N_EP)]
    peers += [fdev(1, 0, 0), fdev(0, 1, 0), fdev(0, 2, 0), fdev(0, 3, 0), fdev(0, 0, 1)]
    for dev in peers:
        pl.semaphore_signal(barrier, inc=1, device_id=dev, device_id_type=MESH)

    own = pl.ds(pl.multiple_of(f * SHARD, SHARD), SHARD)
    w[own, 0:FF] = wg[...]
    w[own, FF:2 * FF] = wu[...]
    w[own, 2 * FF:] = wd[...]

    idt = ids_t[...]
    gpt = gp_t[...].astype(F32)
    chosen, gates = [], []
    for i in range(N_EP):
        match = idt == owner(i, 1)
        chosen.append(jnp.sum(jnp.where(match, 1.0, 0.0), axis=0, keepdims=True))
        gates.append(jnp.sum(jnp.where(match, gpt, 0.0), axis=0, keepdims=True))
    chosen_all = jnp.concatenate(chosen, axis=0)
    before = (
        lax.broadcasted_iota(jnp.int32, (TOK, TOK), 0)
        < lax.broadcasted_iota(jnp.int32, (TOK, TOK), 1)
    )
    place = dot(chosen_all.astype(BF), jnp.where(before, 1.0, 0.0).astype(BF))
    place = jnp.where(chosen_all > 0.5, place, -1.0)
    want = lax.broadcasted_iota(jnp.int32, (MOST, TOK), 0).astype(F32)
    for i in range(N_EP):
        hit = place[i:i + 1, :] == want
        pm[i * MOST:(i + 1) * MOST, :] = jnp.where(hit, 1.0, 0.0).astype(BF)
        gcol = jnp.sum(jnp.where(hit, gates[i], 0.0), axis=1, keepdims=True)
        gc[i * MOST:(i + 1) * MOST, :] = jnp.broadcast_to(gcol, (MOST, 128))

    pl.semaphore_wait(barrier, len(peers))

    send(wrows(f), wrows(f), w_ss.at[0], w_rs.at[0], fdev(1, 0, 0))
    for d in (1, 2, 3):
        send(wrows(f), wrows(f), w_ss.at[d], w_rs.at[d], fdev(0, d, 0))
    send(wrows(f), wrows(f), w_ss.at[7], w_rs.at[7], fdev(0, 0, 1))

    for half in (1, 0):
        rows = slice(half * 256, half * 256 + 256)
        pick = pm[rows, :]
        gcol = gc[rows, 0:1]
        for n in range(4):
            cols = slice(n * 512, n * 512 + 512)
            snd[rows, n * 512:n * 512 + 512] = dot(pick, tok[:, cols]).astype(BF)
            snd[rows, D + n * 512:D + n * 512 + 512] = (
                gcol * dot(pick, og[:, cols])
            ).astype(BF)
        for i in reversed(range(half * 8, half * 8 + 8)):
            part = pl.ds(i * MOST, MOST)
            if i == 0:
                rcv[part, :] = snd[part, :]
            else:
                send(
                    snd.at[part, :], rcv.at[part, :], a_ss.at[i - 1], a_rs.at[i - 1],
                    (f, owner(i, 1)),
                )
        ptm[:, rows] = pick.T

    def arrived(k, fs):
        copy(wrows(fs), wrows(fs), w_ss.at[0], w_rs.at[k], fdev(0, 0, 1)).wait_recv()

    far = fdev(1, 0, 0)[0]
    arrived(0, far)
    for d in (1, 2, 3):
        send(wrows(far), wrows(far), w_ss.at[3 + d], w_rs.at[3 + d], fdev(0, d, 0))
    send(wrows(far), wrows(far), w_ss.at[8], w_rs.at[8], fdev(0, 0, 1))
    for dx, base in ((0, 0), (1, 3)):
        for d in (1, 2, 3):
            fs = fdev(dx, 4 - d, 0)[0]
            arrived(base + d, fs)
            k = 8 + base + d
            send(wrows(fs), wrows(fs), w_ss.at[k], w_rs.at[k], fdev(0, 0, 1))
    arrived(7, fdev(0, 0, 1)[0])
    arrived(8, fdev(1, 0, 1)[0])
    for dx, base in ((0, 0), (1, 3)):
        for d in (1, 2, 3):
            arrived(8 + base + d, fdev(dx, 4 - d, 1)[0])

    for first, count in BLOCKS:
        for i in range(first, first + count):
            if i:
                part = pl.ds(i * MOST, MOST)
                copy(
                    snd.at[part, :], rcv.at[part, :], a_ss.at[i - 1], a_rs.at[i - 1],
                    (f, owner(i, 1)),
                ).wait_recv()
        n_rows = count * MOST
        rows = slice(first * MOST, first * MOST + n_rows)
        xt[:, rows] = rcv[rows, 0:D].T
        qt[:, rows] = rcv[rows, D:].T

        def hidden(n, pick_sum):
            at = pl.multiple_of(n * 256, 256)
            x = rcv[rows, 0:D]
            a = dot(x, w[:, pl.ds(at, 256)])
            b = dot(x, w[:, pl.ds(at + FF, 256)])
            r = dot(rcv[rows, D:], w[:, pl.ds(at + 2 * FF, 256)])
            s = jax.nn.sigmoid(a)
            silu = a * s
            h = (silu * b).astype(BF)
            hh[rows, pl.ds(at, 256)] = h
            dl[rows, pl.ds(at, 256)] = (r * b * s * (1.0 + a * (1.0 - s))).astype(BF)
            dl[rows, pl.ds(at + FF, 256)] = (r * silu).astype(BF)
            return pick_sum + jnp.sum(h.astype(F32) * r, axis=1, keepdims=True)

        pick_sum = lax.fori_loop(0, FF // 256, hidden, jnp.zeros((n_rows, 1), F32))
        cs[rows, D:] = jnp.broadcast_to(pick_sum, (n_rows, 128)).astype(BF)

        def back(m, carry):
            at = pl.multiple_of(m * 256, 256)
            cs[rows, pl.ds(at, 256)] = lax.dot_general(
                dl[rows, :], w[pl.ds(at, 256), 0:2 * FF], (((1,), (1,)), ((), ())),
                preferred_element_type=F32,
            ).astype(BF)
            return carry

        lax.fori_loop(0, D // 256, back, 0)
        for i in range(first, first + count):
            part = pl.ds(i * MOST, MOST)
            if i == 0:
                cr[part, :] = cs[part, :]
            else:
                send(
                    cs.at[part, :], cr.at[part, :], c_ss.at[i - 1], c_rs.at[i - 1],
                    (f, owner(i, -1)),
                )

    mine, other = pl.multiple_of(c * SHARD, SHARD), pl.multiple_of((1 - c) * SHARD, SHARD)

    def reduce_pair(j):
        dx, d = CHIPS[j]
        part = pl.ds(j * SHARD, SHARD)
        copy(
            tb.at[j, pl.ds(other, SHARD), :], sb.at[part, :], s_ss.at[j], s_rs.at[j],
            fdev(0, 0, 1),
        ).wait_recv()
        sb[part, :] = (
            sb[part, :].astype(F32) + tb[j, pl.ds(mine, SHARD), :].astype(F32)
        ).astype(BF)
        if d:
            k = dx * 3 + d - 1
            send(sb.at[part, :], ry.at[k], y_ss.at[k], y_rs.at[k], fdev(0, d, 0))

    for j, (dx, d) in enumerate(CHIPS):
        at = pl.multiple_of((((xh + dx) % 2) * 4 + (y + d) % 4) * 256, 256)
        tb[j, :, 0:2 * FF] = dot(xt[pl.ds(at, 256), :], dl[...]).astype(BF)
        tb[j, :, 2 * FF:] = dot(qt[pl.ds(at, 256), :], hh[...]).astype(BF)
        send(
            tb.at[j, pl.ds(other, SHARD), :], sb.at[pl.ds(j * SHARD, SHARD), :],
            s_ss.at[j], s_rs.at[j], fdev(0, 0, 1),
        )
        if j:
            reduce_pair(j - 1)
    reduce_pair(len(CHIPS) - 1)

    def y_sum(dx):
        j = CHIPS.index((dx, 0))
        total = sb[j * SHARD:(j + 1) * SHARD, :].astype(F32)
        for d in (1, 2, 3):
            k = dx * 3 + d - 1
            copy(ry.at[k], ry.at[k], y_ss.at[k], y_rs.at[k], fdev(0, d, 0)).wait_recv()
            total = total + ry[k].astype(F32)
        return total

    xs[...] = y_sum(1).astype(BF)
    send(xs, rx, x_ss, x_rs, fdev(1, 0, 0))

    lane = lax.broadcasted_iota(jnp.int32, (MOST, 128), 1)
    for i in range(N_EP):
        part = pl.ds(i * MOST, MOST)
        if i:
            copy(
                cs.at[part, :], cr.at[part, :], c_ss.at[i - 1], c_rs.at[i - 1],
                (f, owner(i, -1)),
            ).wait_recv()
        cr[part, D:] = jnp.where(lane == owner(i, 1), cr[part, D:], jnp.zeros((), BF))
    for n in range(4):
        cols = slice(n * 512, n * 512 + 512)
        in_grad[:, cols] = dot(ptm[...], cr[:, cols]).astype(BF)
    picks = dot(ptm[...], cr[:, D:])
    lanes = lax.broadcasted_iota(jnp.int32, (TOK, 128), 1)
    for k in range(8):
        got = jnp.where(ids[:, k:k + 1] == lanes, picks, 0.0)
        gate_grad[:, k:k + 1] = (
            jnp.sum(got, axis=1, keepdims=True) / gp[:, k:k + 1].astype(F32)
        ).astype(BF)

    total = y_sum(0)
    copy(xs, rx, x_ss, x_rs, fdev(1, 0, 0)).wait_recv()
    total = (total + rx[...].astype(F32)).astype(BF)
    gg[...] = total[:, 0:FF]
    gu[...] = total[:, FF:2 * FF]
    gd[...] = total[:, 2 * FF:]
    for cp in sends:
        cp.wait_send()


def per_device(tokens, out_grad, expert_ids, gate_probs, w_gate, w_up, w_down):
    vmem = pl.BlockSpec(memory_space=pltpu.VMEM)
    dma = pltpu.SemaphoreType.DMA
    outs = pl.pallas_call(
        kernel,
        out_shape=(
            jax.ShapeDtypeStruct((TOK, D), BF),
            jax.ShapeDtypeStruct((TOK, 8), BF),
        ) + (jax.ShapeDtypeStruct((SHARD, FF), BF),) * 3,
        in_specs=[vmem] * 9,
        out_specs=(vmem,) * 5,
        scratch_shapes=[
            pltpu.VMEM((D, 3 * FF), BF),
            pltpu.VMEM((ROWS, 2 * D), BF),
            pltpu.VMEM((ROWS, 2 * D), BF),
            pltpu.VMEM((D, ROWS), BF),
            pltpu.VMEM((D, ROWS), BF),
            pltpu.VMEM((ROWS, 2 * FF), BF),
            pltpu.VMEM((ROWS, FF), BF),
            pltpu.VMEM((ROWS, CW), BF),
            pltpu.VMEM((ROWS, CW), BF),
            pltpu.VMEM((8, 256, 3 * FF), BF),
            pltpu.VMEM((8 * SHARD, 3 * FF), BF),
            pltpu.VMEM((6, SHARD, 3 * FF), BF),
            pltpu.VMEM((SHARD, 3 * FF), BF),
            pltpu.VMEM((SHARD, 3 * FF), BF),
            pltpu.VMEM((ROWS, TOK), BF),
            pltpu.VMEM((TOK, ROWS), BF),
            pltpu.VMEM((ROWS, 128), F32),
            dma((15,)), dma((15,)), dma((15,)), dma((15,)), dma((15,)), dma((15,)),
            dma((8,)), dma((8,)), dma((6,)), dma((6,)), dma, dma,
        ],
        compiler_params=pltpu.CompilerParams(
            collective_id=0, has_side_effects=True, vmem_limit_bytes=62 * 2**20
        ),
        name="expert_backward",
    )(
        tokens, out_grad, expert_ids.T, gate_probs.T, expert_ids, gate_probs,
        w_gate[:, 0, :], w_up[:, 0, :], w_down[:, 0, :],
    )
    in_grad, gate_grad, g_gate, g_up, g_down = outs
    return in_grad, gate_grad, g_gate[:, None, :], g_up[:, None, :], g_down[:, None, :]


def solution(mesh):
    rows = P(("fsdp", "ep"), None)
    weight = P("fsdp", "ep", None)
    return jax.shard_map(
        per_device,
        mesh=mesh,
        in_specs=(rows,) * 4 + (weight,) * 3,
        out_specs=(rows,) * 2 + (weight,) * 3,
        check_vma=False,
    )
```

```python
import jax
import jax.numpy as jnp
from jax import lax
from jax.experimental import pallas as pl
from jax.experimental.pallas import tpu as pltpu
from jax.sharding import PartitionSpec as P

MESH = pl.DeviceIdType.MESH
BF = jnp.bfloat16
F32 = jnp.float32

MOST = 32
D = 2048
FF = 768
TOK = 256
N_EP = 16
N_Z = 8
ROWS = N_EP * MOST
SHARD = 128
HALF = SHARD // 2
CW = D + 128

OFFS = (
    (0, 0), (1, 0), (0, 1), (0, 7),
    (1, 1), (1, 7), (0, 2), (0, 6),
    (1, 2), (1, 6), (0, 3), (0, 5),
    (1, 3), (1, 5), (0, 4), (1, 4),
)
BLOCKS = ((0, 8), (8, 4), (12, 4))
CHIPS = ((1, 2), (0, 2), (1, 1), (1, 3), (0, 1), (0, 3), (1, 0), (0, 0))


def dot(a, b):
    return jnp.dot(a, b, preferred_element_type=F32)


def kernel(
    tok, og, ids_t, gp_t, wg, wu, wd,
    in_grad, gate_grad, gg, gu, gd,
    w, snd, rcv, xt, qt, dl, hh, cs, cr, tb, sb, rf, ry, xs, rx, pm, ptm, gc,
    w_ss, w_rs, a_ss, a_rs, c_ss, c_rs, s_ss, s_rs, f_ss, f_rs, y_ss, y_rs, x_ss, x_rs,
):
    f = lax.axis_index("fsdp")
    e = lax.axis_index("ep")
    xh, y, c = f // 8, (f // 2) % 4, f % 2
    xl, z = e // N_Z, e % N_Z
    sends = []

    def fdev(dx, dy, dc):
        return ((((xh + dx) % 2) * 4 + (y + dy) % 4) * 2 + (c + dc) % 2, e)

    def owner(i, sign):
        dx, dz = OFFS[i]
        return ((xl + dx) % 2) * N_Z + (z + N_Z + sign * dz) % N_Z

    def copy(src, dst, ss, rs, dev):
        return pltpu.make_async_remote_copy(
            src_ref=src, dst_ref=dst, send_sem=ss, recv_sem=rs,
            device_id=dev, device_id_type=MESH,
        )

    def send(*args):
        cp = copy(*args)
        cp.start()
        sends.append(cp)

    def wrows(fs):
        return w.at[pl.ds(pl.multiple_of(fs * SHARD, SHARD), SHARD), :]

    barrier = pltpu.get_barrier_semaphore()
    peers = [(f, owner(i, 1)) for i in range(1, N_EP)]
    peers += [fdev(1, 0, 0), fdev(0, 1, 0), fdev(0, 2, 0), fdev(0, 3, 0), fdev(0, 0, 1)]
    for dev in peers:
        pl.semaphore_signal(barrier, inc=1, device_id=dev, device_id_type=MESH)

    own = pl.ds(pl.multiple_of(f * SHARD, SHARD), SHARD)
    w[own, 0:FF] = wg[...]
    w[own, FF:2 * FF] = wu[...]
    w[own, 2 * FF:] = wd[...]

    idt = ids_t[...]
    gpt = gp_t[...].astype(F32)
    chosen, gates = [], []
    for i in range(N_EP):
        match = idt == owner(i, 1)
        chosen.append(jnp.sum(jnp.where(match, 1.0, 0.0), axis=0, keepdims=True))
        gates.append(jnp.sum(jnp.where(match, gpt, 0.0), axis=0, keepdims=True))
    chosen_all = jnp.concatenate(chosen, axis=0)
    before = (
        lax.broadcasted_iota(jnp.int32, (TOK, TOK), 0)
        < lax.broadcasted_iota(jnp.int32, (TOK, TOK), 1)
    )
    place = dot(chosen_all.astype(BF), jnp.where(before, 1.0, 0.0).astype(BF))
    place = jnp.where(chosen_all > 0.5, place, -1.0)
    want = lax.broadcasted_iota(jnp.int32, (MOST, TOK), 0).astype(F32)
    for i in range(N_EP):
        hit = place[i:i + 1, :] == want
        pm[i * MOST:(i + 1) * MOST, :] = jnp.where(hit, 1.0, 0.0).astype(BF)
        gcol = jnp.sum(jnp.where(hit, gates[i], 0.0), axis=1, keepdims=True)
        gc[i * MOST:(i + 1) * MOST, :] = jnp.broadcast_to(gcol, (MOST, 128))

    pl.semaphore_wait(barrier, len(peers))

    send(wrows(f), wrows(f), w_ss.at[0], w_rs.at[0], fdev(1, 0, 0))
    for d in (1, 2, 3):
        send(wrows(f), wrows(f), w_ss.at[d], w_rs.at[d], fdev(0, d, 0))
    send(wrows(f), wrows(f), w_ss.at[7], w_rs.at[7], fdev(0, 0, 1))

    for half in (0, 1):
        rows = slice(half * 256, half * 256 + 256)
        pick = pm[rows, :]
        gcol = gc[rows, 0:1]
        for n in range(4):
            cols = slice(n * 512, n * 512 + 512)
            snd[rows, n * 512:n * 512 + 512] = dot(pick, tok[:, cols]).astype(BF)
            snd[rows, D + n * 512:D + n * 512 + 512] = (
                gcol * dot(pick, og[:, cols])
            ).astype(BF)
        for i in range(half * 8, half * 8 + 8):
            part = pl.ds(i * MOST, MOST)
            if i == 0:
                rcv[part, :] = snd[part, :]
            else:
                send(
                    snd.at[part, :], rcv.at[part, :], a_ss.at[i - 1], a_rs.at[i - 1],
                    (f, owner(i, 1)),
                )
        ptm[:, rows] = pick.T

    def arrived(k, fs):
        copy(wrows(fs), wrows(fs), w_ss.at[0], w_rs.at[k], fdev(0, 0, 1)).wait_recv()

    far = fdev(1, 0, 0)[0]
    arrived(0, far)
    for d in (1, 2, 3):
        send(wrows(far), wrows(far), w_ss.at[3 + d], w_rs.at[3 + d], fdev(0, d, 0))
    send(wrows(far), wrows(far), w_ss.at[8], w_rs.at[8], fdev(0, 0, 1))
    for dx, base in ((0, 0), (1, 3)):
        for d in (1, 2, 3):
            fs = fdev(dx, 4 - d, 0)[0]
            arrived(base + d, fs)
            k = 8 + base + d
            send(wrows(fs), wrows(fs), w_ss.at[k], w_rs.at[k], fdev(0, 0, 1))
    arrived(7, fdev(0, 0, 1)[0])
    arrived(8, fdev(1, 0, 1)[0])
    for dx, base in ((0, 0), (1, 3)):
        for d in (1, 2, 3):
            arrived(8 + base + d, fdev(dx, 4 - d, 1)[0])

    for first, count in BLOCKS:
        for i in range(first, first + count):
            if i:
                part = pl.ds(i * MOST, MOST)
                copy(
                    snd.at[part, :], rcv.at[part, :], a_ss.at[i - 1], a_rs.at[i - 1],
                    (f, owner(i, 1)),
                ).wait_recv()
        n_rows = count * MOST
        rows = slice(first * MOST, first * MOST + n_rows)
        xt[:, rows] = rcv[rows, 0:D].T
        qt[:, rows] = rcv[rows, D:].T

        def hidden(n, pick_sum):
            at = pl.multiple_of(n * 256, 256)
            x = rcv[rows, 0:D]
            a = dot(x, w[:, pl.ds(at, 256)])
            b = dot(x, w[:, pl.ds(at + FF, 256)])
            r = dot(rcv[rows, D:], w[:, pl.ds(at + 2 * FF, 256)])
            s = jax.nn.sigmoid(a)
            silu = a * s
            h = (silu * b).astype(BF)
            hh[rows, pl.ds(at, 256)] = h
            dl[rows, pl.ds(at, 256)] = (r * b * s * (1.0 + a * (1.0 - s))).astype(BF)
            dl[rows, pl.ds(at + FF, 256)] = (r * silu).astype(BF)
            return pick_sum + jnp.sum(h.astype(F32) * r, axis=1, keepdims=True)

        pick_sum = lax.fori_loop(0, FF // 256, hidden, jnp.zeros((n_rows, 1), F32))
        cs[rows, D:] = jnp.broadcast_to(pick_sum, (n_rows, 128)).astype(BF)

        def back(m, carry):
            at = pl.multiple_of(m * 256, 256)
            cs[rows, pl.ds(at, 256)] = lax.dot_general(
                dl[rows, :], w[pl.ds(at, 256), 0:2 * FF], (((1,), (1,)), ((), ())),
                preferred_element_type=F32,
            ).astype(BF)
            return carry

        lax.fori_loop(0, D // 256, back, 0)
        for i in range(first, first + count):
            part = pl.ds(i * MOST, MOST)
            if i == 0:
                cr[part, :] = cs[part, :]
            else:
                send(
                    cs.at[part, :], cr.at[part, :], c_ss.at[i - 1], c_rs.at[i - 1],
                    (f, owner(i, -1)),
                )

    mine, other = pl.multiple_of(c * SHARD, SHARD), pl.multiple_of((1 - c) * SHARD, SHARD)

    def reduce_pair(j):
        dx, d = CHIPS[j]
        part = pl.ds(j * SHARD, SHARD)
        copy(
            tb.at[j, pl.ds(other, SHARD), :], sb.at[part, :], s_ss.at[j], s_rs.at[j],
            fdev(0, 0, 1),
        ).wait_recv()
        for way, step in ((0, 1), (1, 3)):
            half = pl.ds(j * SHARD + way * HALF, HALF)
            total = (
                sb[half, :].astype(F32)
                + tb[j, pl.ds(mine + way * HALF, HALF), :].astype(F32)
            )
            k = dx * 2 + way
            if d == step:
                copy(
                    rf.at[k], rf.at[k], f_ss.at[k], f_rs.at[k], fdev(0, d, 0)
                ).wait_recv()
                total = total + rf[k].astype(F32)
            sb[half, :] = total.astype(BF)
            if d == 2:
                send(sb.at[half, :], rf.at[k], f_ss.at[k], f_rs.at[k], fdev(0, step, 0))
        if d in (1, 3):
            k = dx * 2 + d // 2
            send(sb.at[part, :], ry.at[k], y_ss.at[k], y_rs.at[k], fdev(0, d, 0))

    for j, (dx, d) in enumerate(CHIPS):
        at = pl.multiple_of((((xh + dx) % 2) * 4 + (y + d) % 4) * 256, 256)
        tb[j, :, 0:2 * FF] = dot(xt[pl.ds(at, 256), :], dl[...]).astype(BF)
        tb[j, :, 2 * FF:] = dot(qt[pl.ds(at, 256), :], hh[...]).astype(BF)
        send(
            tb.at[j, pl.ds(other, SHARD), :], sb.at[pl.ds(j * SHARD, SHARD), :],
            s_ss.at[j], s_rs.at[j], fdev(0, 0, 1),
        )
        if j in (1, 2):
            reduce_pair(j - 1)
    for j in range(2, len(CHIPS)):
        reduce_pair(j)

    def y_sum(dx):
        j = CHIPS.index((dx, 0))
        total = sb[j * SHARD:(j + 1) * SHARD, :].astype(F32)
        for k in (2 * dx, 2 * dx + 1):
            copy(ry.at[k], ry.at[k], y_ss.at[k], y_rs.at[k], fdev(0, 1, 0)).wait_recv()
            total = total + ry[k].astype(F32)
        return total

    xs[...] = y_sum(1).astype(BF)
    send(xs, rx, x_ss, x_rs, fdev(1, 0, 0))

    lane = lax.broadcasted_iota(jnp.int32, (MOST, 128), 1)
    for i in range(N_EP):
        part = pl.ds(i * MOST, MOST)
        if i:
            copy(
                cs.at[part, :], cr.at[part, :], c_ss.at[i - 1], c_rs.at[i - 1],
                (f, owner(i, -1)),
            ).wait_recv()
        cr[part, D:] = jnp.where(lane == owner(i, 1), cr[part, D:], jnp.zeros((), BF))
    for n in range(4):
        cols = slice(n * 512, n * 512 + 512)
        in_grad[:, cols] = dot(ptm[...], cr[:, cols]).astype(BF)
    picks = dot(ptm[...], cr[:, D:]).T
    got = jnp.zeros((8, TOK), F32)
    for expert in range(N_EP):
        got = got + jnp.where(idt == expert, picks[expert:expert + 1, :], 0.0)
    gate_grad[...] = (got / gpt).astype(BF)

    total = y_sum(0)
    copy(xs, rx, x_ss, x_rs, fdev(1, 0, 0)).wait_recv()
    total = (total + rx[...].astype(F32)).astype(BF)
    gg[...] = total[:, 0:FF]
    gu[...] = total[:, FF:2 * FF]
    gd[...] = total[:, 2 * FF:]
    for cp in sends:
        cp.wait_send()


def per_device(tokens, out_grad, expert_ids, gate_probs, w_gate, w_up, w_down):
    vmem = pl.BlockSpec(memory_space=pltpu.VMEM)
    dma = pltpu.SemaphoreType.DMA
    outs = pl.pallas_call(
        kernel,
        out_shape=(
            jax.ShapeDtypeStruct((TOK, D), BF),
            jax.ShapeDtypeStruct((8, TOK), BF),
        ) + (jax.ShapeDtypeStruct((SHARD, FF), BF),) * 3,
        in_specs=[vmem] * 7,
        out_specs=(vmem,) * 5,
        scratch_shapes=[
            pltpu.VMEM((D, 3 * FF), BF),
            pltpu.VMEM((ROWS, 2 * D), BF),
            pltpu.VMEM((ROWS, 2 * D), BF),
            pltpu.VMEM((D, ROWS), BF),
            pltpu.VMEM((D, ROWS), BF),
            pltpu.VMEM((ROWS, 2 * FF), BF),
            pltpu.VMEM((ROWS, FF), BF),
            pltpu.VMEM((ROWS, CW), BF),
            pltpu.VMEM((ROWS, CW), BF),
            pltpu.VMEM((8, 256, 3 * FF), BF),
            pltpu.VMEM((8 * SHARD, 3 * FF), BF),
            pltpu.VMEM((4, HALF, 3 * FF), BF),
            pltpu.VMEM((4, SHARD, 3 * FF), BF),
            pltpu.VMEM((SHARD, 3 * FF), BF),
            pltpu.VMEM((SHARD, 3 * FF), BF),
            pltpu.VMEM((ROWS, TOK), BF),
            pltpu.VMEM((TOK, ROWS), BF),
            pltpu.VMEM((ROWS, 128), F32),
            dma((15,)), dma((15,)), dma((15,)), dma((15,)), dma((15,)), dma((15,)),
            dma((8,)), dma((8,)), dma((4,)), dma((4,)), dma((4,)), dma((4,)), dma, dma,
        ],
        compiler_params=pltpu.CompilerParams(
            collective_id=0, has_side_effects=True, vmem_limit_bytes=62 * 2**20
        ),
        name="expert_backward",
    )(
        tokens, out_grad, expert_ids.T, gate_probs.T,
        w_gate[:, 0, :], w_up[:, 0, :], w_down[:, 0, :],
    )
    in_grad, gate_grad, g_gate, g_up, g_down = outs
    return in_grad, gate_grad.T, g_gate[:, None, :], g_up[:, None, :], g_down[:, None, :]


def solution(mesh):
    rows = P(("fsdp", "ep"), None)
    weight = P("fsdp", "ep", None)
    return jax.shard_map(
        per_device,
        mesh=mesh,
        in_specs=(rows,) * 4 + (weight,) * 3,
        out_specs=(rows,) * 2 + (weight,) * 3,
        check_vma=False,
    )
```

```python
import jax
import jax.numpy as jnp
from jax import lax
from jax.experimental import pallas as pl
from jax.experimental.pallas import tpu as pltpu
from jax.sharding import PartitionSpec as P

MESH = pl.DeviceIdType.MESH
BF = jnp.bfloat16
F32 = jnp.float32

MOST = 32
D = 2048
FF = 768
TOK = 256
N_EP = 16
N_Z = 8
ROWS = N_EP * MOST
SHARD = 128
HALF = SHARD // 2
CW = D + 128

OFFS = (
    (0, 0), (1, 0), (0, 1), (0, 7),
    (1, 1), (1, 7), (0, 2), (0, 6),
    (1, 2), (1, 6), (0, 3), (0, 5),
    (1, 3), (1, 5), (0, 4), (1, 4),
)
BLOCKS = ((0, 8), (8, 4), (12, 4))
CHIPS = ((1, 2), (0, 2), (1, 1), (1, 3), (0, 1), (0, 3), (1, 0), (0, 0))


def dot(a, b):
    return jnp.dot(a, b, preferred_element_type=F32)


def kernel(
    tok_in, og_in, ids_t, gp_t, wg, wu, wd,
    in_grad, gate_grad, gg, gu, gd,
    tok, og, w, snd, rcv, xt, qt, dl, hh, cs, cr, tb, sb, rf, ry, xs, rx, pm, ptm, gc,
    w_ss, w_rs, a_ss, a_rs, c_ss, c_rs, s_ss, s_rs, f_ss, f_rs, y_ss, y_rs, x_ss, x_rs, l_s,
):
    f = lax.axis_index("fsdp")
    e = lax.axis_index("ep")
    xh, y, c = f // 8, (f // 2) % 4, f % 2
    xl, z = e // N_Z, e % N_Z
    sends = []

    def fdev(dx, dy, dc):
        return ((((xh + dx) % 2) * 4 + (y + dy) % 4) * 2 + (c + dc) % 2, e)

    def owner(i, sign):
        dx, dz = OFFS[i]
        return ((xl + dx) % 2) * N_Z + (z + N_Z + sign * dz) % N_Z

    def copy(src, dst, ss, rs, dev):
        return pltpu.make_async_remote_copy(
            src_ref=src, dst_ref=dst, send_sem=ss, recv_sem=rs,
            device_id=dev, device_id_type=MESH,
        )

    def send(*args):
        cp = copy(*args)
        cp.start()
        sends.append(cp)

    def wrows(fs):
        return w.at[pl.ds(pl.multiple_of(fs * SHARD, SHARD), SHARD), :]

    own = pl.ds(pl.multiple_of(f * SHARD, SHARD), SHARD)
    loads = [
        pltpu.make_async_copy(tok_in, tok, l_s.at[0]),
        pltpu.make_async_copy(og_in, og, l_s.at[1]),
        pltpu.make_async_copy(wg, w.at[own, 0:FF], l_s.at[2]),
        pltpu.make_async_copy(wu, w.at[own, FF:2 * FF], l_s.at[3]),
        pltpu.make_async_copy(wd, w.at[own, 2 * FF:], l_s.at[4]),
    ]
    for cp in loads:
        cp.start()

    barrier = pltpu.get_barrier_semaphore()
    peers = [(f, owner(i, 1)) for i in range(1, N_EP)]
    peers += [fdev(1, 0, 0), fdev(0, 1, 0), fdev(0, 2, 0), fdev(0, 3, 0), fdev(0, 0, 1)]
    for dev in peers:
        pl.semaphore_signal(barrier, inc=1, device_id=dev, device_id_type=MESH)


    idt = ids_t[...]
    gpt = gp_t[...].astype(F32)
    chosen, gates = [], []
    for i in range(N_EP):
        match = idt == owner(i, 1)
        chosen.append(jnp.sum(jnp.where(match, 1.0, 0.0), axis=0, keepdims=True))
        gates.append(jnp.sum(jnp.where(match, gpt, 0.0), axis=0, keepdims=True))
    chosen_all = jnp.concatenate(chosen, axis=0)
    before = (
        lax.broadcasted_iota(jnp.int32, (TOK, TOK), 0)
        < lax.broadcasted_iota(jnp.int32, (TOK, TOK), 1)
    )
    place = dot(chosen_all.astype(BF), jnp.where(before, 1.0, 0.0).astype(BF))
    place = jnp.where(chosen_all > 0.5, place, -1.0)
    want = lax.broadcasted_iota(jnp.int32, (MOST, TOK), 0).astype(F32)
    for i in range(N_EP):
        hit = place[i:i + 1, :] == want
        pm[i * MOST:(i + 1) * MOST, :] = jnp.where(hit, 1.0, 0.0).astype(BF)
        gcol = jnp.sum(jnp.where(hit, gates[i], 0.0), axis=1, keepdims=True)
        gc[i * MOST:(i + 1) * MOST, :] = jnp.broadcast_to(gcol, (MOST, 128))

    def gather(half):
        rows = slice(half * 256, half * 256 + 256)
        pick = pm[rows, :]
        gcol = gc[rows, 0:1]
        for n in range(4):
            cols = slice(n * 512, n * 512 + 512)
            snd[rows, n * 512:n * 512 + 512] = dot(pick, tok[:, cols]).astype(BF)
            snd[rows, D + n * 512:D + n * 512 + 512] = (
                gcol * dot(pick, og[:, cols])
            ).astype(BF)

    def dispatch(half):
        for i in range(half * 8, half * 8 + 8):
            part = pl.ds(i * MOST, MOST)
            if i:
                send(
                    snd.at[part, :], rcv.at[part, :], a_ss.at[i - 1], a_rs.at[i - 1],
                    (f, owner(i, 1)),
                )

    for cp in loads:
        cp.wait()
    gather(0)
    pl.semaphore_wait(barrier, len(peers))

    send(wrows(f), wrows(f), w_ss.at[0], w_rs.at[0], fdev(1, 0, 0))
    for d in (1, 2, 3):
        send(wrows(f), wrows(f), w_ss.at[d], w_rs.at[d], fdev(0, d, 0))
    send(wrows(f), wrows(f), w_ss.at[7], w_rs.at[7], fdev(0, 0, 1))

    dispatch(0)
    gather(1)
    dispatch(1)
    rcv[0:MOST, :] = snd[0:MOST, :]
    for half in (0, 1):
        ptm[:, half * 256:half * 256 + 256] = pm[half * 256:half * 256 + 256, :].T

    def arrived(k, fs):
        copy(wrows(fs), wrows(fs), w_ss.at[0], w_rs.at[k], fdev(0, 0, 1)).wait_recv()

    far = fdev(1, 0, 0)[0]
    arrived(0, far)
    for d in (1, 2, 3):
        send(wrows(far), wrows(far), w_ss.at[3 + d], w_rs.at[3 + d], fdev(0, d, 0))
    send(wrows(far), wrows(far), w_ss.at[8], w_rs.at[8], fdev(0, 0, 1))
    for dx, base in ((0, 0), (1, 3)):
        for d in (1, 2, 3):
            fs = fdev(dx, 4 - d, 0)[0]
            arrived(base + d, fs)
            k = 8 + base + d
            send(wrows(fs), wrows(fs), w_ss.at[k], w_rs.at[k], fdev(0, 0, 1))
    arrived(7, fdev(0, 0, 1)[0])
    arrived(8, fdev(1, 0, 1)[0])
    for dx, base in ((0, 0), (1, 3)):
        for d in (1, 2, 3):
            arrived(8 + base + d, fdev(dx, 4 - d, 1)[0])

    def block_rows(first, count):
        return slice(first * MOST, (first + count) * MOST)

    def forward(first, count):
        rows = block_rows(first, count)
        xt[:, rows] = rcv[rows, 0:D].T
        qt[:, rows] = rcv[rows, D:].T

        def hidden(n, pick_sum):
            at = pl.multiple_of(n * 256, 256)
            x = rcv[rows, 0:D]
            a = dot(x, w[:, pl.ds(at, 256)])
            b = dot(x, w[:, pl.ds(at + FF, 256)])
            r = dot(rcv[rows, D:], w[:, pl.ds(at + 2 * FF, 256)])
            s = jax.nn.sigmoid(a)
            silu = a * s
            h = (silu * b).astype(BF)
            hh[rows, pl.ds(at, 256)] = h
            dl[rows, pl.ds(at, 256)] = (r * b * s * (1.0 + a * (1.0 - s))).astype(BF)
            dl[rows, pl.ds(at + FF, 256)] = (r * silu).astype(BF)
            return pick_sum + jnp.sum(h.astype(F32) * r, axis=1, keepdims=True)

        pick_sum = lax.fori_loop(
            0, FF // 256, hidden, jnp.zeros((count * MOST, 1), F32)
        )
        cs[rows, D:] = jnp.broadcast_to(pick_sum, (count * MOST, 128)).astype(BF)

    def backward(first, count):
        rows = block_rows(first, count)

        def back(m, carry):
            at = pl.multiple_of(m * 256, 256)
            cs[rows, pl.ds(at, 256)] = lax.dot_general(
                dl[rows, :], w[pl.ds(at, 256), 0:2 * FF], (((1,), (1,)), ((), ())),
                preferred_element_type=F32,
            ).astype(BF)
            return carry

        lax.fori_loop(0, D // 256, back, 0)

    def give_back(first, count):
        for i in range(first, first + count):
            part = pl.ds(i * MOST, MOST)
            if i == 0:
                cr[part, :] = cs[part, :]
            else:
                send(
                    cs.at[part, :], cr.at[part, :], c_ss.at[i - 1], c_rs.at[i - 1],
                    (f, owner(i, -1)),
                )

    last = BLOCKS[-1]
    for block in BLOCKS:
        for i in range(block[0], block[0] + block[1]):
            if i:
                part = pl.ds(i * MOST, MOST)
                copy(
                    snd.at[part, :], rcv.at[part, :], a_ss.at[i - 1], a_rs.at[i - 1],
                    (f, owner(i, 1)),
                ).wait_recv()
        if block is last:
            for earlier in BLOCKS[:-1]:
                give_back(*earlier)
        forward(*block)
        if block is not last:
            backward(*block)

    mine, other = pl.multiple_of(c * SHARD, SHARD), pl.multiple_of((1 - c) * SHARD, SHARD)

    def reduce_pair(j):
        dx, d = CHIPS[j]
        part = pl.ds(j * SHARD, SHARD)
        copy(
            tb.at[j, pl.ds(other, SHARD), :], sb.at[part, :], s_ss.at[j], s_rs.at[j],
            fdev(0, 0, 1),
        ).wait_recv()
        for way, step in ((0, 1), (1, 3)):
            half = pl.ds(j * SHARD + way * HALF, HALF)
            total = (
                sb[half, :].astype(F32)
                + tb[j, pl.ds(mine + way * HALF, HALF), :].astype(F32)
            )
            k = dx * 2 + way
            if d == step:
                copy(
                    rf.at[k], rf.at[k], f_ss.at[k], f_rs.at[k], fdev(0, d, 0)
                ).wait_recv()
                total = total + rf[k].astype(F32)
            sb[half, :] = total.astype(BF)
            if d == 2:
                send(sb.at[half, :], rf.at[k], f_ss.at[k], f_rs.at[k], fdev(0, step, 0))
        if d in (1, 3):
            k = dx * 2 + d // 2
            send(sb.at[part, :], ry.at[k], y_ss.at[k], y_rs.at[k], fdev(0, d, 0))

    for j, (dx, d) in enumerate(CHIPS):
        at = pl.multiple_of((((xh + dx) % 2) * 4 + (y + d) % 4) * 256, 256)
        tb[j, :, 0:2 * FF] = dot(xt[pl.ds(at, 256), :], dl[...]).astype(BF)
        tb[j, :, 2 * FF:] = dot(qt[pl.ds(at, 256), :], hh[...]).astype(BF)
        send(
            tb.at[j, pl.ds(other, SHARD), :], sb.at[pl.ds(j * SHARD, SHARD), :],
            s_ss.at[j], s_rs.at[j], fdev(0, 0, 1),
        )
        if j in (1, 2):
            reduce_pair(j - 1)
    backward(*last)
    give_back(*last)
    for j in range(2, len(CHIPS)):
        reduce_pair(j)

    def y_sum(dx):
        j = CHIPS.index((dx, 0))
        total = sb[j * SHARD:(j + 1) * SHARD, :].astype(F32)
        for k in (2 * dx, 2 * dx + 1):
            copy(ry.at[k], ry.at[k], y_ss.at[k], y_rs.at[k], fdev(0, 1, 0)).wait_recv()
            total = total + ry[k].astype(F32)
        return total

    xs[...] = y_sum(1).astype(BF)
    send(xs, rx, x_ss, x_rs, fdev(1, 0, 0))

    lane = lax.broadcasted_iota(jnp.int32, (MOST, 128), 1)
    for i in range(N_EP):
        part = pl.ds(i * MOST, MOST)
        if i:
            copy(
                cs.at[part, :], cr.at[part, :], c_ss.at[i - 1], c_rs.at[i - 1],
                (f, owner(i, -1)),
            ).wait_recv()
        cr[part, D:] = jnp.where(lane == owner(i, 1), cr[part, D:], jnp.zeros((), BF))
    for n in range(4):
        cols = slice(n * 512, n * 512 + 512)
        tok[:, cols] = dot(ptm[...], cr[:, cols]).astype(BF)
    store = pltpu.make_async_copy(tok, in_grad, l_s.at[5])
    store.start()
    picks = dot(ptm[...], cr[:, D:]).T
    got = jnp.zeros((8, TOK), F32)
    for expert in range(N_EP):
        got = got + jnp.where(idt == expert, picks[expert:expert + 1, :], 0.0)
    gate_grad[...] = (got / gpt).astype(BF)

    total = y_sum(0)
    copy(xs, rx, x_ss, x_rs, fdev(1, 0, 0)).wait_recv()
    total = (total + rx[...].astype(F32)).astype(BF)
    gg[...] = total[:, 0:FF]
    gu[...] = total[:, FF:2 * FF]
    gd[...] = total[:, 2 * FF:]
    store.wait()
    for cp in sends:
        cp.wait_send()


def per_device(tokens, out_grad, expert_ids, gate_probs, w_gate, w_up, w_down):
    vmem = pl.BlockSpec(memory_space=pltpu.VMEM)
    hbm = pl.BlockSpec(memory_space=pl.ANY)
    dma = pltpu.SemaphoreType.DMA
    outs = pl.pallas_call(
        kernel,
        out_shape=(
            jax.ShapeDtypeStruct((TOK, D), BF),
            jax.ShapeDtypeStruct((8, TOK), BF),
        ) + (jax.ShapeDtypeStruct((SHARD, FF), BF),) * 3,
        in_specs=[hbm, hbm, vmem, vmem, hbm, hbm, hbm],
        out_specs=(hbm,) + (vmem,) * 4,
        scratch_shapes=[
            pltpu.VMEM((TOK, D), BF),
            pltpu.VMEM((TOK, D), BF),
            pltpu.VMEM((D, 3 * FF), BF),
            pltpu.VMEM((ROWS, 2 * D), BF),
            pltpu.VMEM((ROWS, 2 * D), BF),
            pltpu.VMEM((D, ROWS), BF),
            pltpu.VMEM((D, ROWS), BF),
            pltpu.VMEM((ROWS, 2 * FF), BF),
            pltpu.VMEM((ROWS, FF), BF),
            pltpu.VMEM((ROWS, CW), BF),
            pltpu.VMEM((ROWS, CW), BF),
            pltpu.VMEM((8, 256, 3 * FF), BF),
            pltpu.VMEM((8 * SHARD, 3 * FF), BF),
            pltpu.VMEM((4, HALF, 3 * FF), BF),
            pltpu.VMEM((4, SHARD, 3 * FF), BF),
            pltpu.VMEM((SHARD, 3 * FF), BF),
            pltpu.VMEM((SHARD, 3 * FF), BF),
            pltpu.VMEM((ROWS, TOK), BF),
            pltpu.VMEM((TOK, ROWS), BF),
            pltpu.VMEM((ROWS, 128), F32),
            dma((15,)), dma((15,)), dma((15,)), dma((15,)), dma((15,)), dma((15,)),
            dma((8,)), dma((8,)), dma((4,)), dma((4,)), dma((4,)), dma((4,)), dma, dma, dma((6,)),
        ],
        compiler_params=pltpu.CompilerParams(
            collective_id=0, has_side_effects=True, vmem_limit_bytes=62 * 2**20
        ),
        name="expert_backward",
    )(
        tokens, out_grad, expert_ids.T, gate_probs.T,
        w_gate[:, 0, :], w_up[:, 0, :], w_down[:, 0, :],
    )
    in_grad, gate_grad, g_gate, g_up, g_down = outs
    return in_grad, gate_grad.T, g_gate[:, None, :], g_up[:, None, :], g_down[:, None, :]


def solution(mesh):
    rows = P(("fsdp", "ep"), None)
    weight = P("fsdp", "ep", None)
    return jax.shard_map(
        per_device,
        mesh=mesh,
        in_specs=(rows,) * 4 + (weight,) * 3,
        out_specs=(rows,) * 2 + (weight,) * 3,
        check_vma=False,
    )
```

```python
import jax
import jax.numpy as jnp
from jax import lax
from jax.experimental import pallas as pl
from jax.experimental.pallas import tpu as pltpu
from jax.sharding import PartitionSpec as P

MESH = pl.DeviceIdType.MESH
BF = jnp.bfloat16
F32 = jnp.float32

MOST = 32
D = 2048
FF = 768
TOK = 256
N_EP = 16
N_Z = 8
ROWS = N_EP * MOST
SHARD = 128
HALF = SHARD // 2

OFFS = (
    (0, 0), (1, 0), (0, 1), (0, 7),
    (1, 1), (1, 7), (0, 2), (0, 6),
    (1, 2), (1, 6), (0, 3), (0, 5),
    (1, 3), (1, 5), (0, 4), (1, 4),
)
BLOCKS = ((0, 8), (8, 4), (12, 4))
CHIPS = ((1, 2), (0, 2), (1, 1), (1, 3), (0, 1), (0, 3), (1, 0), (0, 0))


def dot(a, b):
    return jnp.dot(a, b, preferred_element_type=F32)


def kernel(
    tok_in, og_in, ids_t, gp_t, wg, wu, wd,
    in_grad, gate_grad, grads,
    tok, og, w, snd, rcv, xt, qt, dl, hh, cs, cr, ps, pr, pv, tb, sb, rf, ry, xs, rx, pm, ptm, gc,
    w_ss, w_rs, a_ss, a_rs, c_ss, c_rs, p_ss, p_rs, s_ss, s_rs, f_ss, f_rs, y_ss, y_rs, x_ss, x_rs, l_s,
):
    f = lax.axis_index("fsdp")
    e = lax.axis_index("ep")
    xh, y, c = f // 8, (f // 2) % 4, f % 2
    xl, z = e // N_Z, e % N_Z
    sends = []

    def fdev(dx, dy, dc):
        return ((((xh + dx) % 2) * 4 + (y + dy) % 4) * 2 + (c + dc) % 2, e)

    def owner(i, sign):
        dx, dz = OFFS[i]
        return ((xl + dx) % 2) * N_Z + (z + N_Z + sign * dz) % N_Z

    def copy(src, dst, ss, rs, dev):
        return pltpu.make_async_remote_copy(
            src_ref=src, dst_ref=dst, send_sem=ss, recv_sem=rs,
            device_id=dev, device_id_type=MESH,
        )

    def send(*args):
        cp = copy(*args)
        cp.start()
        sends.append(cp)

    def wrows(fs):
        return w.at[pl.ds(pl.multiple_of(fs * SHARD, SHARD), SHARD), :]

    own = pl.ds(pl.multiple_of(f * SHARD, SHARD), SHARD)
    loads = [
        pltpu.make_async_copy(tok_in, tok, l_s.at[0]),
        pltpu.make_async_copy(og_in, og, l_s.at[1]),
        pltpu.make_async_copy(wg, w.at[own, 0:FF], l_s.at[2]),
        pltpu.make_async_copy(wu, w.at[own, FF:2 * FF], l_s.at[3]),
        pltpu.make_async_copy(wd, w.at[own, 2 * FF:], l_s.at[4]),
    ]
    for cp in loads:
        cp.start()

    barrier = pltpu.get_barrier_semaphore()
    peers = [(f, owner(i, 1)) for i in range(1, N_EP)]
    peers += [fdev(1, 0, 0), fdev(0, 1, 0), fdev(0, 2, 0), fdev(0, 3, 0), fdev(0, 0, 1)]
    for dev in peers:
        pl.semaphore_signal(barrier, inc=1, device_id=dev, device_id_type=MESH)


    idt = ids_t[...]
    gpt = gp_t[...].astype(F32)
    chosen, gates = [], []
    for i in range(N_EP):
        match = idt == owner(i, 1)
        chosen.append(jnp.sum(jnp.where(match, 1.0, 0.0), axis=0, keepdims=True))
        gates.append(jnp.sum(jnp.where(match, gpt, 0.0), axis=0, keepdims=True))
    chosen_all = jnp.concatenate(chosen, axis=0)
    before = (
        lax.broadcasted_iota(jnp.int32, (TOK, TOK), 0)
        < lax.broadcasted_iota(jnp.int32, (TOK, TOK), 1)
    )
    place = dot(chosen_all.astype(BF), jnp.where(before, 1.0, 0.0).astype(BF))
    place = jnp.where(chosen_all > 0.5, place, -1.0)
    want = lax.broadcasted_iota(jnp.int32, (MOST, TOK), 0).astype(F32)
    for i in range(N_EP):
        hit = place[i:i + 1, :] == want
        pm[i * MOST:(i + 1) * MOST, :] = jnp.where(hit, 1.0, 0.0).astype(BF)
        gcol = jnp.sum(jnp.where(hit, gates[i], 0.0), axis=1, keepdims=True)
        gc[i * MOST:(i + 1) * MOST, :] = jnp.broadcast_to(gcol, (MOST, 128))

    def gather(half):
        rows = slice(half * 256, half * 256 + 256)
        pick = pm[rows, :]
        gcol = gc[rows, 0:1]
        for n in range(4):
            cols = slice(n * 512, n * 512 + 512)
            snd[rows, n * 512:n * 512 + 512] = dot(pick, tok[:, cols]).astype(BF)
            snd[rows, D + n * 512:D + n * 512 + 512] = (
                gcol * dot(pick, og[:, cols])
            ).astype(BF)

    def dispatch(half):
        for i in range(half * 8, half * 8 + 8):
            part = pl.ds(i * MOST, MOST)
            if i:
                send(
                    snd.at[part, :], rcv.at[part, :], a_ss.at[i - 1], a_rs.at[i - 1],
                    (f, owner(i, 1)),
                )

    for cp in loads:
        cp.wait()
    gather(0)
    pl.semaphore_wait(barrier, len(peers))

    send(wrows(f), wrows(f), w_ss.at[0], w_rs.at[0], fdev(1, 0, 0))
    for d in (1, 2, 3):
        send(wrows(f), wrows(f), w_ss.at[d], w_rs.at[d], fdev(0, d, 0))
    send(wrows(f), wrows(f), w_ss.at[7], w_rs.at[7], fdev(0, 0, 1))

    dispatch(0)
    gather(1)
    dispatch(1)
    rcv[0:MOST, :] = snd[0:MOST, :]
    for half in (0, 1):
        ptm[:, half * 256:half * 256 + 256] = pm[half * 256:half * 256 + 256, :].T

    def arrived(k, fs):
        copy(wrows(fs), wrows(fs), w_ss.at[0], w_rs.at[k], fdev(0, 0, 1)).wait_recv()

    far = fdev(1, 0, 0)[0]
    arrived(0, far)
    for d in (1, 2, 3):
        send(wrows(far), wrows(far), w_ss.at[3 + d], w_rs.at[3 + d], fdev(0, d, 0))
    send(wrows(far), wrows(far), w_ss.at[8], w_rs.at[8], fdev(0, 0, 1))
    for dx, base in ((0, 0), (1, 3)):
        for d in (1, 2, 3):
            fs = fdev(dx, 4 - d, 0)[0]
            arrived(base + d, fs)
            k = 8 + base + d
            send(wrows(fs), wrows(fs), w_ss.at[k], w_rs.at[k], fdev(0, 0, 1))
    arrived(7, fdev(0, 0, 1)[0])
    arrived(8, fdev(1, 0, 1)[0])
    for dx, base in ((0, 0), (1, 3)):
        for d in (1, 2, 3):
            arrived(8 + base + d, fdev(dx, 4 - d, 1)[0])

    def block_rows(first, count):
        return slice(first * MOST, (first + count) * MOST)

    def forward(first, count):
        rows = block_rows(first, count)

        def hidden(n, pick_sum):
            at = pl.multiple_of(n * 256, 256)
            third = pl.multiple_of(n * 640, 128)
            xt[pl.ds(third, FF), rows] = rcv[rows, pl.ds(third, FF)].T
            qt[pl.ds(third, FF), rows] = rcv[rows, pl.ds(D + third, FF)].T
            x = rcv[rows, 0:D]
            a = dot(x, w[:, pl.ds(at, 256)])
            b = dot(x, w[:, pl.ds(at + FF, 256)])
            r = dot(rcv[rows, D:], w[:, pl.ds(at + 2 * FF, 256)])
            s = jax.nn.sigmoid(a)
            silu = a * s
            h = (silu * b).astype(BF)
            hh[rows, pl.ds(at, 256)] = h
            dl[rows, pl.ds(at, 256)] = (r * b * s * (1.0 + a * (1.0 - s))).astype(BF)
            dl[rows, pl.ds(at + FF, 256)] = (r * silu).astype(BF)
            return pick_sum + jnp.sum(h.astype(F32) * r, axis=1, keepdims=True)

        pick_sum = lax.fori_loop(
            0, FF // 256, hidden, jnp.zeros((count * MOST, 1), F32)
        )
        ps[:, rows] = jnp.broadcast_to(pick_sum, (count * MOST, 128)).T[0:16, :].astype(BF)

    def backward(first, count):
        rows = block_rows(first, count)

        def back(m, carry):
            at = pl.multiple_of(m * 256, 256)
            cs[rows, pl.ds(at, 256)] = lax.dot_general(
                dl[rows, :], w[pl.ds(at, 256), 0:2 * FF], (((1,), (1,)), ((), ())),
                preferred_element_type=F32,
            ).astype(BF)
            return carry

        lax.fori_loop(0, D // 256, back, 0)

    def give_back(first, count):
        for i in range(first, first + count):
            part = pl.ds(i * MOST, MOST)
            four = pl.ds(i // 4 * 128, 128)
            if i == 0:
                cr[part, :] = cs[part, :]
                pr[0] = ps[:, four]
            else:
                dev = (f, owner(i, -1))
                send(cs.at[part, :], cr.at[part, :], c_ss.at[i - 1], c_rs.at[i - 1], dev)
                send(ps.at[:, four], pr.at[i], p_ss.at[i - 1], p_rs.at[i - 1], dev)

    last = BLOCKS[-1]
    for block in BLOCKS:
        for i in range(block[0], block[0] + block[1]):
            if i:
                part = pl.ds(i * MOST, MOST)
                copy(
                    snd.at[part, :], rcv.at[part, :], a_ss.at[i - 1], a_rs.at[i - 1],
                    (f, owner(i, 1)),
                ).wait_recv()
        if block is last:
            give_back(*BLOCKS[0])
        forward(*block)
        if block is not last:
            backward(*block)

    mine, other = pl.multiple_of(c * SHARD, SHARD), pl.multiple_of((1 - c) * SHARD, SHARD)

    def reduce_pair(j):
        dx, d = CHIPS[j]
        part = pl.ds(j * SHARD, SHARD)
        copy(
            tb.at[j, pl.ds(other, SHARD), :], sb.at[part, :], s_ss.at[j], s_rs.at[j],
            fdev(0, 0, 1),
        ).wait_recv()
        for way, step in ((0, 1), (1, 3)):
            half = pl.ds(j * SHARD + way * HALF, HALF)
            total = (
                sb[half, :].astype(F32)
                + tb[j, pl.ds(mine + way * HALF, HALF), :].astype(F32)
            )
            k = dx * 2 + way
            if d == step:
                copy(
                    rf.at[k], rf.at[k], f_ss.at[k], f_rs.at[k], fdev(0, d, 0)
                ).wait_recv()
                total = total + rf[k].astype(F32)
            sb[half, :] = total.astype(BF)
            if d == 2:
                send(sb.at[half, :], rf.at[k], f_ss.at[k], f_rs.at[k], fdev(0, step, 0))
        if d in (1, 3):
            k = dx * 2 + d // 2
            send(sb.at[part, :], ry.at[k], y_ss.at[k], y_rs.at[k], fdev(0, d, 0))

    for j, (dx, d) in enumerate(CHIPS):
        at = pl.multiple_of((((xh + dx) % 2) * 4 + (y + d) % 4) * 256, 256)
        tb[j, :, 0:2 * FF] = dot(xt[pl.ds(at, 256), :], dl[...]).astype(BF)
        tb[j, :, 2 * FF:] = dot(qt[pl.ds(at, 256), :], hh[...]).astype(BF)
        send(
            tb.at[j, pl.ds(other, SHARD), :], sb.at[pl.ds(j * SHARD, SHARD), :],
            s_ss.at[j], s_rs.at[j], fdev(0, 0, 1),
        )
        if j in (1, 2):
            reduce_pair(j - 1)
            if j == 1:
                give_back(*BLOCKS[1])
    backward(*last)
    give_back(*last)
    for j in range(2, len(CHIPS)):
        reduce_pair(j)

    def y_sum(dx):
        j = CHIPS.index((dx, 0))
        total = sb[j * SHARD:(j + 1) * SHARD, :].astype(F32)
        for k in (2 * dx, 2 * dx + 1):
            copy(ry.at[k], ry.at[k], y_ss.at[k], y_rs.at[k], fdev(0, 1, 0)).wait_recv()
            total = total + ry[k].astype(F32)
        return total

    xs[...] = y_sum(1).astype(BF)
    send(xs, rx, x_ss, x_rs, fdev(1, 0, 0))

    lane = lax.broadcasted_iota(jnp.int32, (1, ROWS), 1)
    for i in range(N_EP):
        part = pl.ds(i * MOST, MOST)
        four = pl.ds(i // 4 * 128, 128)
        if i:
            dev = (f, owner(i, -1))
            copy(
                cs.at[part, :], cr.at[part, :], c_ss.at[i - 1], c_rs.at[i - 1], dev
            ).wait_recv()
            copy(ps.at[:, four], pr.at[i], p_ss.at[i - 1], p_rs.at[i - 1], dev).wait_recv()
        row = jnp.concatenate([pr[i, 0:1, :].astype(F32)] * 4, axis=1)
        pv[i:i + 1, :] = jnp.where(lane // MOST == i, row, 0.0)
    for n in range(4):
        cols = slice(n * 512, n * 512 + 512)
        tok[:, cols] = dot(ptm[...], cr[:, cols]).astype(BF)
    store = pltpu.make_async_copy(tok, in_grad, l_s.at[5])
    store.start()
    picks = dot(pv[...].astype(BF), pm[...])
    got = jnp.zeros((8, TOK), F32)
    for i in range(N_EP):
        got = got + jnp.where(idt == owner(i, 1), picks[i:i + 1, :], 0.0)
    gate_grad[...] = (got / gpt).astype(BF)

    total = y_sum(0)
    copy(xs, rx, x_ss, x_rs, fdev(1, 0, 0)).wait_recv()
    total = (total + rx[...].astype(F32)).astype(BF)
    grads[...] = total
    store.wait()
    for cp in sends:
        cp.wait_send()


def hand_over(
    in_grad, gate_grad, grads, in_out, gate_out, gg, gu, gd, in_buf, gate_buf, g_buf,
    load_sems, store_sems,
):
    loads = [(in_grad.at[n * 64:n * 64 + 64, :], in_buf.at[n * 64:n * 64 + 64, :]) for n in range(4)]
    loads += [(grads.at[:, n * FF:(n + 1) * FF], g_buf.at[n]) for n in range(3)]
    loads += [(gate_grad, gate_buf)]
    stores = [(in_buf.at[n * 64:n * 64 + 64, :], in_out.at[n * 64:n * 64 + 64, :]) for n in range(4)]
    stores += [(g_buf.at[n], g) for n, g in enumerate((gg, gu, gd))]
    stores += [(gate_buf, gate_out)]
    loads = [
        pltpu.make_async_copy(src, dst, load_sems.at[n]) for n, (src, dst) in enumerate(loads)
    ]
    stores = [
        pltpu.make_async_copy(src, dst, store_sems.at[n]) for n, (src, dst) in enumerate(stores)
    ]
    for cp in loads:
        cp.start()
    for load, store in zip(loads, stores):
        load.wait()
        store.start()
    for cp in stores:
        cp.wait()


def per_device(tokens, out_grad, expert_ids, gate_probs, w_gate, w_up, w_down):
    vmem = pl.BlockSpec(memory_space=pltpu.VMEM)
    hbm = pl.BlockSpec(memory_space=pl.ANY)
    dma = pltpu.SemaphoreType.DMA
    outs = pl.pallas_call(
        kernel,
        out_shape=(
            jax.ShapeDtypeStruct((TOK, D), BF),
            jax.ShapeDtypeStruct((8, TOK), BF),
            jax.ShapeDtypeStruct((SHARD, 3 * FF), BF),
        ),
        in_specs=[hbm, hbm, vmem, vmem, hbm, hbm, hbm],
        out_specs=(hbm, vmem, vmem),
        scratch_shapes=[
            pltpu.VMEM((TOK, D), BF),
            pltpu.VMEM((TOK, D), BF),
            pltpu.VMEM((D, 3 * FF), BF),
            pltpu.VMEM((ROWS, 2 * D), BF),
            pltpu.VMEM((ROWS, 2 * D), BF),
            pltpu.VMEM((D, ROWS), BF),
            pltpu.VMEM((D, ROWS), BF),
            pltpu.VMEM((ROWS, 2 * FF), BF),
            pltpu.VMEM((ROWS, FF), BF),
            pltpu.VMEM((ROWS, D), BF),
            pltpu.VMEM((ROWS, D), BF),
            pltpu.VMEM((16, ROWS), BF),
            pltpu.VMEM((N_EP, 16, 128), BF),
            pltpu.VMEM((N_EP, ROWS), F32),
            pltpu.VMEM((8, 256, 3 * FF), BF),
            pltpu.VMEM((8 * SHARD, 3 * FF), BF),
            pltpu.VMEM((4, HALF, 3 * FF), BF),
            pltpu.VMEM((4, SHARD, 3 * FF), BF),
            pltpu.VMEM((SHARD, 3 * FF), BF),
            pltpu.VMEM((SHARD, 3 * FF), BF),
            pltpu.VMEM((ROWS, TOK), BF),
            pltpu.VMEM((TOK, ROWS), BF),
            pltpu.VMEM((ROWS, 128), F32),
            dma((15,)), dma((15,)), dma((15,)), dma((15,)), dma((15,)), dma((15,)),
            dma((15,)), dma((15,)),
            dma((8,)), dma((8,)), dma((4,)), dma((4,)), dma((4,)), dma((4,)), dma, dma, dma((6,)),
        ],
        compiler_params=pltpu.CompilerParams(
            collective_id=0, has_side_effects=True, vmem_limit_bytes=62 * 2**20
        ),
        name="expert_backward",
    )(
        tokens, out_grad, expert_ids.T, gate_probs.T,
        w_gate[:, 0, :], w_up[:, 0, :], w_down[:, 0, :],
    )
    finish = pl.pallas_call(
        hand_over,
        out_shape=(
            jax.ShapeDtypeStruct((TOK, D), BF),
            jax.ShapeDtypeStruct((8, TOK), BF),
        ) + (jax.ShapeDtypeStruct((SHARD, FF), BF),) * 3,
        in_specs=[hbm] * 3,
        out_specs=(hbm,) * 5,
        scratch_shapes=[
            pltpu.VMEM((TOK, D), BF),
            pltpu.VMEM((8, TOK), BF),
            pltpu.VMEM((3, SHARD, FF), BF),
            dma((8,)), dma((8,)),
        ],
        name="hand_over",
    )
    in_grad, gate_grad, g_gate, g_up, g_down = finish(*outs)
    return in_grad, gate_grad.T, g_gate[:, None, :], g_up[:, None, :], g_down[:, None, :]


def solution(mesh):
    rows = P(("fsdp", "ep"), None)
    weight = P("fsdp", "ep", None)
    return jax.shard_map(
        per_device,
        mesh=mesh,
        in_specs=(rows,) * 4 + (weight,) * 3,
        out_specs=(rows,) * 2 + (weight,) * 3,
        check_vma=False,
    )
```

```python
import jax
import jax.numpy as jnp
from jax import lax
from jax.experimental import pallas as pl
from jax.experimental.pallas import tpu as pltpu
from jax.sharding import PartitionSpec as P

MESH = pl.DeviceIdType.MESH
BF = jnp.bfloat16
F32 = jnp.float32

MOST = 32
D = 2048
FF = 768
TOK = 256
N_EP = 16
N_Z = 8
ROWS = N_EP * MOST
SHARD = 128
HALF = SHARD // 2

OFFS = (
    (0, 0), (1, 0), (0, 1), (0, 7),
    (1, 1), (1, 7), (0, 2), (0, 6),
    (1, 2), (1, 6), (0, 3), (0, 5),
    (1, 5), (1, 3), (1, 4), (0, 4),
)
BLOCKS = ((0, 8), (8, 4), (12, 4))
CHIPS = ((1, 2), (0, 2), (1, 1), (1, 3), (0, 1), (0, 3), (1, 0), (0, 0))

AFTER = ((), (0,), (1,), (), (2,), (3,), (4, 5), (6, 7))


def dot(a, b):
    return jnp.dot(a, b, preferred_element_type=F32)


def kernel(
    tok_in, og_in, ids_t, gp_t, wg, wu, wd,
    in_grad, gate_grad, grads,
    tok, og, w, wt, snd, rcv, xt, qt, dl, hh, cs, cr, ps, pr, pv, tb, sb, rf, ry, xs, rx, pm, ptm, gc,
    w_ss, w_rs, a_ss, a_rs, c_ss, c_rs, p_ss, p_rs, s_ss, s_rs, f_ss, f_rs, y_ss, y_rs, x_ss, x_rs, l_s,
):
    f = lax.axis_index("fsdp")
    e = lax.axis_index("ep")
    xh, y, c = f // 8, (f // 2) % 4, f % 2
    xl, z = e // N_Z, e % N_Z
    sends = []

    def fdev(dx, dy, dc):
        return ((((xh + dx) % 2) * 4 + (y + dy) % 4) * 2 + (c + dc) % 2, e)

    def owner(i, sign):
        dx, dz = OFFS[i]
        return ((xl + dx) % 2) * N_Z + (z + N_Z + sign * dz) % N_Z

    def copy(src, dst, ss, rs, dev):
        return pltpu.make_async_remote_copy(
            src_ref=src, dst_ref=dst, send_sem=ss, recv_sem=rs,
            device_id=dev, device_id_type=MESH,
        )

    def send(*args):
        cp = copy(*args)
        cp.start()
        sends.append(cp)

    def wrows(fs):
        return w.at[pl.ds(pl.multiple_of(fs * SHARD, SHARD), SHARD), :]

    own = pl.ds(pl.multiple_of(f * SHARD, SHARD), SHARD)
    loads = [
        pltpu.make_async_copy(tok_in, tok, l_s.at[0]),
        pltpu.make_async_copy(og_in, og, l_s.at[1]),
        pltpu.make_async_copy(wg, w.at[own, 0:FF], l_s.at[2]),
        pltpu.make_async_copy(wu, w.at[own, FF:2 * FF], l_s.at[3]),
        pltpu.make_async_copy(wd, w.at[own, 2 * FF:], l_s.at[4]),
    ]
    for cp in loads:
        cp.start()

    barrier = pltpu.get_barrier_semaphore()
    peers = [(f, owner(i, 1)) for i in range(1, N_EP)]
    peers += [fdev(1, 0, 0), fdev(0, 1, 0), fdev(0, 2, 0), fdev(0, 3, 0), fdev(0, 0, 1)]
    for dev in peers:
        pl.semaphore_signal(barrier, inc=1, device_id=dev, device_id_type=MESH)


    idt = ids_t[...]
    gpt = gp_t[...].astype(F32)
    chosen, gates = [], []
    for i in range(N_EP):
        match = idt == owner(i, 1)
        chosen.append(jnp.sum(jnp.where(match, 1.0, 0.0), axis=0, keepdims=True))
        gates.append(jnp.sum(jnp.where(match, gpt, 0.0), axis=0, keepdims=True))
    chosen_all = jnp.concatenate(chosen, axis=0)
    before = (
        lax.broadcasted_iota(jnp.int32, (TOK, TOK), 0)
        < lax.broadcasted_iota(jnp.int32, (TOK, TOK), 1)
    )
    place = dot(chosen_all.astype(BF), jnp.where(before, 1.0, 0.0).astype(BF))
    place = jnp.where(chosen_all > 0.5, place, -1.0)
    want = lax.broadcasted_iota(jnp.int32, (MOST, TOK), 0).astype(F32)
    for i in range(N_EP):
        hit = place[i:i + 1, :] == want
        pm[i * MOST:(i + 1) * MOST, :] = jnp.where(hit, 1.0, 0.0).astype(BF)
        gcol = jnp.sum(jnp.where(hit, gates[i], 0.0), axis=1, keepdims=True)
        gc[i * MOST:(i + 1) * MOST, :] = jnp.broadcast_to(gcol, (MOST, 128))

    def gather(half):
        rows = slice(half * 256, half * 256 + 256)
        pick = pm[rows, :]
        gcol = gc[rows, 0:1]
        for n in range(4):
            cols = slice(n * 512, n * 512 + 512)
            snd[rows, n * 512:n * 512 + 512] = dot(pick, tok[:, cols]).astype(BF)
            snd[rows, D + n * 512:D + n * 512 + 512] = (
                gcol * dot(pick, og[:, cols])
            ).astype(BF)

    def dispatch(half):
        for i in range(half * 8, half * 8 + 8):
            part = pl.ds(i * MOST, MOST)
            if i:
                send(
                    snd.at[part, :], rcv.at[part, :], a_ss.at[i - 1], a_rs.at[i - 1],
                    (f, owner(i, 1)),
                )

    for cp in loads:
        cp.wait()
    gather(0)
    pl.semaphore_wait(barrier, len(peers))

    send(wrows(f), wrows(f), w_ss.at[0], w_rs.at[0], fdev(1, 0, 0))
    for d in (1, 2, 3):
        send(wrows(f), wrows(f), w_ss.at[d], w_rs.at[d], fdev(0, d, 0))
    send(wrows(f), wrows(f), w_ss.at[7], w_rs.at[7], fdev(0, 0, 1))

    dispatch(0)
    gather(1)
    dispatch(1)
    rcv[0:MOST, :] = snd[0:MOST, :]
    for half in (0, 1):
        ptm[:, half * 256:half * 256 + 256] = pm[half * 256:half * 256 + 256, :].T

    def turn(fs):
        at = pl.multiple_of(fs * SHARD, SHARD)
        wt[:, pl.ds(at, SHARD)] = w[pl.ds(at, SHARD), 0:2 * FF].T

    turn(f)

    def arrived(k, fs):
        copy(wrows(fs), wrows(fs), w_ss.at[0], w_rs.at[k], fdev(0, 0, 1)).wait_recv()

    far = fdev(1, 0, 0)[0]
    arrived(0, far)
    for d in (1, 2, 3):
        send(wrows(far), wrows(far), w_ss.at[3 + d], w_rs.at[3 + d], fdev(0, d, 0))
    send(wrows(far), wrows(far), w_ss.at[8], w_rs.at[8], fdev(0, 0, 1))
    turn(far)
    for dx, base in ((0, 0), (1, 3)):
        for d in (1, 2, 3):
            fs = fdev(dx, 4 - d, 0)[0]
            arrived(base + d, fs)
            k = 8 + base + d
            send(wrows(fs), wrows(fs), w_ss.at[k], w_rs.at[k], fdev(0, 0, 1))
            turn(fs)
    for k in (0, 1):
        fs = fdev(k, 0, 1)[0]
        arrived(7 + k, fs)
        turn(fs)
    for dx, base in ((0, 0), (1, 3)):
        for d in (1, 2, 3):
            fs = fdev(dx, 4 - d, 1)[0]
            arrived(8 + base + d, fs)
            turn(fs)

    def block_rows(first, count):
        return slice(first * MOST, (first + count) * MOST)

    def forward(first, count):
        rows = block_rows(first, count)

        def hidden(n, pick_sum):
            at = pl.multiple_of(n * 256, 256)
            third = pl.multiple_of(n * 640, 128)
            xt[pl.ds(third, FF), rows] = rcv[rows, pl.ds(third, FF)].T
            qt[pl.ds(third, FF), rows] = rcv[rows, pl.ds(D + third, FF)].T
            x = rcv[rows, 0:D]
            a = dot(x, w[:, pl.ds(at, 256)])
            b = dot(x, w[:, pl.ds(at + FF, 256)])
            r = dot(rcv[rows, D:], w[:, pl.ds(at + 2 * FF, 256)])
            s = jax.nn.sigmoid(a)
            silu = a * s
            h = (silu * b).astype(BF)
            hh[rows, pl.ds(at, 256)] = h
            dl[rows, pl.ds(at, 256)] = (r * b * s * (1.0 + a * (1.0 - s))).astype(BF)
            dl[rows, pl.ds(at + FF, 256)] = (r * silu).astype(BF)
            return pick_sum + jnp.sum(h.astype(F32) * r, axis=1, keepdims=True)

        pick_sum = lax.fori_loop(
            0, FF // 256, hidden, jnp.zeros((count * MOST, 1), F32)
        )
        ps[:, rows] = jnp.broadcast_to(pick_sum, (count * MOST, 128)).T[0:16, :].astype(BF)

    def backward(first, count):
        rows = block_rows(first, count)

        def back(m, carry):
            at = pl.multiple_of(m * 256, 256)
            cs[rows, pl.ds(at, 256)] = dot(dl[rows, :], wt[:, pl.ds(at, 256)]).astype(BF)
            return carry

        lax.fori_loop(0, D // 256, back, 0)

    def give_back(first, count):
        for i in range(first, first + count):
            part = pl.ds(i * MOST, MOST)
            if i == 0:
                cr[part, :] = cs[part, :]
            else:
                dev = (f, owner(i, -1))
                send(cs.at[part, :], cr.at[part, :], c_ss.at[i - 1], c_rs.at[i - 1], dev)

    def give_picks_back():
        pr[0] = ps[:, 0:128]
        for i in range(1, N_EP):
            four = pl.ds(i // 4 * 128, 128)
            send(
                ps.at[:, four], pr.at[i], p_ss.at[i - 1], p_rs.at[i - 1],
                (f, owner(i, -1)),
            )

    last = BLOCKS[-1]
    for block in BLOCKS:
        for i in range(block[0], block[0] + block[1]):
            if i:
                part = pl.ds(i * MOST, MOST)
                copy(
                    snd.at[part, :], rcv.at[part, :], a_ss.at[i - 1], a_rs.at[i - 1],
                    (f, owner(i, 1)),
                ).wait_recv()
        if block is last:
            for earlier in BLOCKS[:-1]:
                give_back(*earlier)
        forward(*block)
        if block is not last:
            backward(*block)

    mine, other = pl.multiple_of(c * SHARD, SHARD), pl.multiple_of((1 - c) * SHARD, SHARD)

    def reduce_pair(j):
        dx, d = CHIPS[j]
        part = pl.ds(j * SHARD, SHARD)
        copy(
            tb.at[j, pl.ds(other, SHARD), :], sb.at[part, :], s_ss.at[j], s_rs.at[j],
            fdev(0, 0, 1),
        ).wait_recv()
        for way, step in ((0, 1), (1, 3)):
            half = pl.ds(j * SHARD + way * HALF, HALF)
            total = (
                sb[half, :].astype(F32)
                + tb[j, pl.ds(mine + way * HALF, HALF), :].astype(F32)
            )
            k = dx * 2 + way
            if d == step:
                copy(
                    rf.at[k], rf.at[k], f_ss.at[k], f_rs.at[k], fdev(0, d, 0)
                ).wait_recv()
                total = total + rf[k].astype(F32)
            sb[half, :] = total.astype(BF)
            if d == 2:
                send(sb.at[half, :], rf.at[k], f_ss.at[k], f_rs.at[k], fdev(0, step, 0))
        if d in (1, 3):
            k = dx * 2 + d // 2
            send(sb.at[part, :], ry.at[k], y_ss.at[k], y_rs.at[k], fdev(0, d, 0))

    for j, (dx, d) in enumerate(CHIPS):
        at = pl.multiple_of((((xh + dx) % 2) * 4 + (y + d) % 4) * 256, 256)
        tb[j, :, 0:2 * FF] = dot(xt[pl.ds(at, 256), :], dl[...]).astype(BF)
        tb[j, :, 2 * FF:] = dot(qt[pl.ds(at, 256), :], hh[...]).astype(BF)
        send(
            tb.at[j, pl.ds(other, SHARD), :], sb.at[pl.ds(j * SHARD, SHARD), :],
            s_ss.at[j], s_rs.at[j], fdev(0, 0, 1),
        )
        for ready in AFTER[j]:
            reduce_pair(ready)
        if j == 3:
            backward(*last)
            give_back(*last)
            give_picks_back()

    def y_sum(dx):
        j = CHIPS.index((dx, 0))
        total = sb[j * SHARD:(j + 1) * SHARD, :].astype(F32)
        for k in (2 * dx, 2 * dx + 1):
            copy(ry.at[k], ry.at[k], y_ss.at[k], y_rs.at[k], fdev(0, 1, 0)).wait_recv()
            total = total + ry[k].astype(F32)
        return total

    xs[...] = y_sum(1).astype(BF)
    send(xs, rx, x_ss, x_rs, fdev(1, 0, 0))

    lane = lax.broadcasted_iota(jnp.int32, (1, ROWS), 1)
    for i in range(N_EP):
        part = pl.ds(i * MOST, MOST)
        four = pl.ds(i // 4 * 128, 128)
        if i:
            dev = (f, owner(i, -1))
            copy(
                cs.at[part, :], cr.at[part, :], c_ss.at[i - 1], c_rs.at[i - 1], dev
            ).wait_recv()
            copy(ps.at[:, four], pr.at[i], p_ss.at[i - 1], p_rs.at[i - 1], dev).wait_recv()
        row = jnp.concatenate([pr[i, 0:1, :].astype(F32)] * 4, axis=1)
        pv[i:i + 1, :] = jnp.where(lane // MOST == i, row, 0.0)
    for n in range(4):
        cols = slice(n * 512, n * 512 + 512)
        tok[:, cols] = dot(ptm[...], cr[:, cols]).astype(BF)
    store = pltpu.make_async_copy(tok, in_grad, l_s.at[5])
    store.start()
    picks = dot(pv[...].astype(BF), pm[...])
    got = jnp.zeros((8, TOK), F32)
    for i in range(N_EP):
        got = got + jnp.where(idt == owner(i, 1), picks[i:i + 1, :], 0.0)
    gate_grad[...] = (got / gpt).astype(BF)

    total = y_sum(0)
    copy(xs, rx, x_ss, x_rs, fdev(1, 0, 0)).wait_recv()
    total = (total + rx[...].astype(F32)).astype(BF)
    grads[...] = total
    store.wait()
    for cp in sends:
        cp.wait_send()


def hand_over(
    in_grad, gate_grad, grads, in_out, gate_out, gg, gu, gd, in_buf, gate_buf, g_buf,
    load_sems, store_sems,
):
    loads = [(in_grad.at[n * 64:n * 64 + 64, :], in_buf.at[n * 64:n * 64 + 64, :]) for n in range(4)]
    loads += [(grads.at[:, n * FF:(n + 1) * FF], g_buf.at[n]) for n in range(3)]
    loads += [(gate_grad, gate_buf)]
    stores = [(in_buf.at[n * 64:n * 64 + 64, :], in_out.at[n * 64:n * 64 + 64, :]) for n in range(4)]
    stores += [(g_buf.at[n], g) for n, g in enumerate((gg, gu, gd))]
    stores += [(gate_buf, gate_out)]
    loads = [
        pltpu.make_async_copy(src, dst, load_sems.at[n]) for n, (src, dst) in enumerate(loads)
    ]
    stores = [
        pltpu.make_async_copy(src, dst, store_sems.at[n]) for n, (src, dst) in enumerate(stores)
    ]
    for cp in loads:
        cp.start()
    for load, store in zip(loads, stores):
        load.wait()
        store.start()
    for cp in stores:
        cp.wait()


def per_device(tokens, out_grad, expert_ids, gate_probs, w_gate, w_up, w_down):
    vmem = pl.BlockSpec(memory_space=pltpu.VMEM)
    hbm = pl.BlockSpec(memory_space=pl.ANY)
    dma = pltpu.SemaphoreType.DMA
    outs = pl.pallas_call(
        kernel,
        out_shape=(
            jax.ShapeDtypeStruct((TOK, D), BF),
            jax.ShapeDtypeStruct((8, TOK), BF),
            jax.ShapeDtypeStruct((SHARD, 3 * FF), BF),
        ),
        in_specs=[hbm, hbm, vmem, vmem, hbm, hbm, hbm],
        out_specs=(hbm, vmem, vmem),
        scratch_shapes=[
            pltpu.VMEM((TOK, D), BF),
            pltpu.VMEM((TOK, D), BF),
            pltpu.VMEM((D, 3 * FF), BF),
            pltpu.VMEM((2 * FF, D), BF),
            pltpu.VMEM((ROWS, 2 * D), BF),
            pltpu.VMEM((ROWS, 2 * D), BF),
            pltpu.VMEM((D, ROWS), BF),
            pltpu.VMEM((D, ROWS), BF),
            pltpu.VMEM((ROWS, 2 * FF), BF),
            pltpu.VMEM((ROWS, FF), BF),
            pltpu.VMEM((ROWS, D), BF),
            pltpu.VMEM((ROWS, D), BF),
            pltpu.VMEM((16, ROWS), BF),
            pltpu.VMEM((N_EP, 16, 128), BF),
            pltpu.VMEM((N_EP, ROWS), F32),
            pltpu.VMEM((8, 256, 3 * FF), BF),
            pltpu.VMEM((8 * SHARD, 3 * FF), BF),
            pltpu.VMEM((4, HALF, 3 * FF), BF),
            pltpu.VMEM((4, SHARD, 3 * FF), BF),
            pltpu.VMEM((SHARD, 3 * FF), BF),
            pltpu.VMEM((SHARD, 3 * FF), BF),
            pltpu.VMEM((ROWS, TOK), BF),
            pltpu.VMEM((TOK, ROWS), BF),
            pltpu.VMEM((ROWS, 128), F32),
            dma((15,)), dma((15,)), dma((15,)), dma((15,)), dma((15,)), dma((15,)),
            dma((15,)), dma((15,)),
            dma((8,)), dma((8,)), dma((4,)), dma((4,)), dma((4,)), dma((4,)), dma, dma, dma((6,)),
        ],
        compiler_params=pltpu.CompilerParams(
            collective_id=0, has_side_effects=True, vmem_limit_bytes=62 * 2**20
        ),
        name="expert_backward",
    )(
        tokens, out_grad, expert_ids.T, gate_probs.T,
        w_gate[:, 0, :], w_up[:, 0, :], w_down[:, 0, :],
    )
    finish = pl.pallas_call(
        hand_over,
        out_shape=(
            jax.ShapeDtypeStruct((TOK, D), BF),
            jax.ShapeDtypeStruct((8, TOK), BF),
        ) + (jax.ShapeDtypeStruct((SHARD, FF), BF),) * 3,
        in_specs=[hbm] * 3,
        out_specs=(hbm,) * 5,
        scratch_shapes=[
            pltpu.VMEM((TOK, D), BF),
            pltpu.VMEM((8, TOK), BF),
            pltpu.VMEM((3, SHARD, FF), BF),
            dma((8,)), dma((8,)),
        ],
        name="hand_over",
    )
    in_grad, gate_grad, g_gate, g_up, g_down = finish(*outs)
    return in_grad, gate_grad.T, g_gate[:, None, :], g_up[:, None, :], g_down[:, None, :]


def solution(mesh):
    rows = P(("fsdp", "ep"), None)
    weight = P("fsdp", "ep", None)
    return jax.shard_map(
        per_device,
        mesh=mesh,
        in_specs=(rows,) * 4 + (weight,) * 3,
        out_specs=(rows,) * 2 + (weight,) * 3,
        check_vma=False,
    )
```

```python
import jax
import jax.numpy as jnp
from jax import lax
from jax.experimental import pallas as pl
from jax.experimental.pallas import tpu as pltpu
from jax.sharding import PartitionSpec as P

MESH = pl.DeviceIdType.MESH
BF = jnp.bfloat16
F32 = jnp.float32

MOST = 32
D = 2048
FF = 768
TOK = 256
N_EP = 16
N_Z = 8
ROWS = N_EP * MOST
SHARD = 128
HALF = SHARD // 2

OFFS = (
    (0, 0), (1, 0), (0, 1), (0, 7),
    (1, 1), (1, 7), (0, 2), (0, 6),
    (1, 6), (1, 2), (0, 5), (0, 3),
    (1, 5), (1, 3), (1, 4), (0, 4),
)
BLOCKS = ((0, 8), (8, 4), (12, 4))
CHIPS = ((1, 2), (0, 2), (1, 1), (1, 3), (0, 1), (0, 3), (1, 0), (0, 0))

AFTER = ((), (0,), (1,), (), (2,), (3,), (4, 5), (6, 7))


def dot(a, b):
    return jnp.dot(a, b, preferred_element_type=F32)


def kernel(
    tok_in, og_in, ids_t, gp_t, wg, wu, wd,
    in_grad, gate_grad, grads,
    tok, og, w, wt, snd, rcv, xt, qt, dl, hh, cs, cr, ps, pr, pv, tb, sb, rf, ry, xs, rx, pm, ptm, gc,
    w_ss, w_rs, a_ss, a_rs, c_ss, c_rs, p_ss, p_rs, s_ss, s_rs, f_ss, f_rs, y_ss, y_rs, x_ss, x_rs, l_s,
):
    f = lax.axis_index("fsdp")
    e = lax.axis_index("ep")
    xh, y, c = f // 8, (f // 2) % 4, f % 2
    xl, z = e // N_Z, e % N_Z
    sends = []

    def fdev(dx, dy, dc):
        return ((((xh + dx) % 2) * 4 + (y + dy) % 4) * 2 + (c + dc) % 2, e)

    def owner(i, sign):
        dx, dz = OFFS[i]
        return ((xl + dx) % 2) * N_Z + (z + N_Z + sign * dz) % N_Z

    def copy(src, dst, ss, rs, dev):
        return pltpu.make_async_remote_copy(
            src_ref=src, dst_ref=dst, send_sem=ss, recv_sem=rs,
            device_id=dev, device_id_type=MESH,
        )

    def send(*args):
        cp = copy(*args)
        cp.start()
        sends.append(cp)

    def wrows(fs):
        return w.at[pl.ds(pl.multiple_of(fs * SHARD, SHARD), SHARD), :]

    own = pl.ds(pl.multiple_of(f * SHARD, SHARD), SHARD)
    loads = [
        pltpu.make_async_copy(tok_in, tok, l_s.at[0]),
        pltpu.make_async_copy(og_in, og, l_s.at[1]),
        pltpu.make_async_copy(wg, w.at[own, 0:FF], l_s.at[2]),
        pltpu.make_async_copy(wu, w.at[own, FF:2 * FF], l_s.at[3]),
        pltpu.make_async_copy(wd, w.at[own, 2 * FF:], l_s.at[4]),
    ]
    for cp in loads:
        cp.start()

    barrier = pltpu.get_barrier_semaphore()
    peers = [(f, owner(i, 1)) for i in range(1, N_EP)]
    peers += [fdev(1, 0, 0), fdev(0, 1, 0), fdev(0, 2, 0), fdev(0, 3, 0), fdev(0, 0, 1)]
    for dev in peers:
        pl.semaphore_signal(barrier, inc=1, device_id=dev, device_id_type=MESH)


    idt = ids_t[...]
    gpt = gp_t[...].astype(F32)
    chosen, gates = [], []
    for i in range(N_EP):
        match = idt == owner(i, 1)
        chosen.append(jnp.sum(jnp.where(match, 1.0, 0.0), axis=0, keepdims=True))
        gates.append(jnp.sum(jnp.where(match, gpt, 0.0), axis=0, keepdims=True))
    chosen_all = jnp.concatenate(chosen, axis=0)
    before = (
        lax.broadcasted_iota(jnp.int32, (TOK, TOK), 0)
        < lax.broadcasted_iota(jnp.int32, (TOK, TOK), 1)
    )
    place = dot(chosen_all.astype(BF), jnp.where(before, 1.0, 0.0).astype(BF))
    place = jnp.where(chosen_all > 0.5, place, -1.0)
    want = lax.broadcasted_iota(jnp.int32, (MOST, TOK), 0).astype(F32)
    for i in range(N_EP):
        hit = place[i:i + 1, :] == want
        pm[i * MOST:(i + 1) * MOST, :] = jnp.where(hit, 1.0, 0.0).astype(BF)
        gcol = jnp.sum(jnp.where(hit, gates[i], 0.0), axis=1, keepdims=True)
        gc[i * MOST:(i + 1) * MOST, :] = jnp.broadcast_to(gcol, (MOST, 128))

    def gather(half):
        rows = slice(half * 256, half * 256 + 256)
        pick = pm[rows, :]
        gcol = gc[rows, 0:1]
        for n in range(4):
            cols = slice(n * 512, n * 512 + 512)
            snd[rows, n * 512:n * 512 + 512] = dot(pick, tok[:, cols]).astype(BF)
            snd[rows, D + n * 512:D + n * 512 + 512] = (
                gcol * dot(pick, og[:, cols])
            ).astype(BF)

    def dispatch(half):
        for i in range(half * 8, half * 8 + 8):
            part = pl.ds(i * MOST, MOST)
            if i:
                send(
                    snd.at[part, :], rcv.at[part, :], a_ss.at[i - 1], a_rs.at[i - 1],
                    (f, owner(i, 1)),
                )

    for cp in loads:
        cp.wait()
    gather(0)
    pl.semaphore_wait(barrier, len(peers))

    send(wrows(f), wrows(f), w_ss.at[0], w_rs.at[0], fdev(1, 0, 0))
    for d in (1, 2, 3):
        send(wrows(f), wrows(f), w_ss.at[d], w_rs.at[d], fdev(0, d, 0))
    send(wrows(f), wrows(f), w_ss.at[7], w_rs.at[7], fdev(0, 0, 1))

    dispatch(0)
    gather(1)
    dispatch(1)
    rcv[0:MOST, :] = snd[0:MOST, :]
    for half in (0, 1):
        ptm[:, half * 256:half * 256 + 256] = pm[half * 256:half * 256 + 256, :].T

    def turn(fs):
        at = pl.multiple_of(fs * SHARD, SHARD)
        wt[:, pl.ds(at, SHARD)] = w[pl.ds(at, SHARD), 0:2 * FF].T

    turn(f)

    def arrived(k, fs):
        copy(wrows(fs), wrows(fs), w_ss.at[0], w_rs.at[k], fdev(0, 0, 1)).wait_recv()

    far = fdev(1, 0, 0)[0]
    arrived(0, far)
    for d in (1, 2, 3):
        send(wrows(far), wrows(far), w_ss.at[3 + d], w_rs.at[3 + d], fdev(0, d, 0))
    send(wrows(far), wrows(far), w_ss.at[8], w_rs.at[8], fdev(0, 0, 1))
    turn(far)
    for dx, base in ((0, 0), (1, 3)):
        for d in (1, 2, 3):
            fs = fdev(dx, 4 - d, 0)[0]
            arrived(base + d, fs)
            k = 8 + base + d
            send(wrows(fs), wrows(fs), w_ss.at[k], w_rs.at[k], fdev(0, 0, 1))
            turn(fs)
    for k in (0, 1):
        fs = fdev(k, 0, 1)[0]
        arrived(7 + k, fs)
        turn(fs)
    for dx, base in ((0, 0), (1, 3)):
        for d in (1, 2, 3):
            fs = fdev(dx, 4 - d, 1)[0]
            arrived(8 + base + d, fs)
            turn(fs)

    def block_rows(first, count):
        return slice(first * MOST, (first + count) * MOST)

    def forward(first, count):
        rows = block_rows(first, count)

        def hidden(n, pick_sum):
            at = pl.multiple_of(n * 256, 256)
            third = pl.multiple_of(n * 640, 128)
            xt[pl.ds(third, FF), rows] = rcv[rows, pl.ds(third, FF)].T
            qt[pl.ds(third, FF), rows] = rcv[rows, pl.ds(D + third, FF)].T
            x = rcv[rows, 0:D]
            a = dot(x, w[:, pl.ds(at, 256)])
            b = dot(x, w[:, pl.ds(at + FF, 256)])
            r = dot(rcv[rows, D:], w[:, pl.ds(at + 2 * FF, 256)])
            s = jax.nn.sigmoid(a)
            silu = a * s
            h = (silu * b).astype(BF)
            hh[rows, pl.ds(at, 256)] = h
            dl[rows, pl.ds(at, 256)] = (r * b * s * (1.0 + a * (1.0 - s))).astype(BF)
            dl[rows, pl.ds(at + FF, 256)] = (r * silu).astype(BF)
            return pick_sum + jnp.sum(h.astype(F32) * r, axis=1, keepdims=True)

        pick_sum = lax.fori_loop(
            0, FF // 256, hidden, jnp.zeros((count * MOST, 1), F32)
        )
        ps[:, rows] = jnp.broadcast_to(pick_sum, (count * MOST, 128)).T[0:16, :].astype(BF)

    def backward(first, count):
        rows = block_rows(first, count)

        def back(m, carry):
            at = pl.multiple_of(m * 256, 256)
            cs[rows, pl.ds(at, 256)] = dot(dl[rows, :], wt[:, pl.ds(at, 256)]).astype(BF)
            return carry

        lax.fori_loop(0, D // 256, back, 0)

    def give_back(first, count):
        for i in range(first, first + count):
            part = pl.ds(i * MOST, MOST)
            if i == 0:
                cr[part, :] = cs[part, :]
            else:
                dev = (f, owner(i, -1))
                send(cs.at[part, :], cr.at[part, :], c_ss.at[i - 1], c_rs.at[i - 1], dev)

    def give_picks_back():
        pr[0] = ps[:, 0:128]
        for i in range(1, N_EP):
            four = pl.ds(i // 4 * 128, 128)
            send(
                ps.at[:, four], pr.at[i], p_ss.at[i - 1], p_rs.at[i - 1],
                (f, owner(i, -1)),
            )

    last = BLOCKS[-1]
    for block in BLOCKS:
        for i in range(block[0], block[0] + block[1]):
            if i:
                part = pl.ds(i * MOST, MOST)
                copy(
                    snd.at[part, :], rcv.at[part, :], a_ss.at[i - 1], a_rs.at[i - 1],
                    (f, owner(i, 1)),
                ).wait_recv()
        if block is last:
            for earlier in BLOCKS[:-1]:
                give_back(*earlier)
        forward(*block)
        if block is not last:
            backward(*block)

    mine, other = pl.multiple_of(c * SHARD, SHARD), pl.multiple_of((1 - c) * SHARD, SHARD)

    def reduce_pair(j):
        dx, d = CHIPS[j]
        part = pl.ds(j * SHARD, SHARD)
        copy(
            tb.at[j, pl.ds(other, SHARD), :], sb.at[part, :], s_ss.at[j], s_rs.at[j],
            fdev(0, 0, 1),
        ).wait_recv()
        for way, step in ((0, 1), (1, 3)):
            half = pl.ds(j * SHARD + way * HALF, HALF)
            total = (
                sb[half, :].astype(F32)
                + tb[j, pl.ds(mine + way * HALF, HALF), :].astype(F32)
            )
            k = dx * 2 + way
            if d == step:
                copy(
                    rf.at[k], rf.at[k], f_ss.at[k], f_rs.at[k], fdev(0, d, 0)
                ).wait_recv()
                total = total + rf[k].astype(F32)
            sb[half, :] = total.astype(BF)
            if d == 2:
                send(sb.at[half, :], rf.at[k], f_ss.at[k], f_rs.at[k], fdev(0, step, 0))
        if d in (1, 3):
            k = dx * 2 + d // 2
            send(sb.at[part, :], ry.at[k], y_ss.at[k], y_rs.at[k], fdev(0, d, 0))

    for j, (dx, d) in enumerate(CHIPS):
        at = pl.multiple_of((((xh + dx) % 2) * 4 + (y + d) % 4) * 256, 256)
        tb[j, :, 0:2 * FF] = dot(xt[pl.ds(at, 256), :], dl[...]).astype(BF)
        tb[j, :, 2 * FF:] = dot(qt[pl.ds(at, 256), :], hh[...]).astype(BF)
        send(
            tb.at[j, pl.ds(other, SHARD), :], sb.at[pl.ds(j * SHARD, SHARD), :],
            s_ss.at[j], s_rs.at[j], fdev(0, 0, 1),
        )
        for ready in AFTER[j]:
            reduce_pair(ready)
        if j == 3:
            backward(*last)
            give_back(*last)
            give_picks_back()

    def y_sum(dx):
        j = CHIPS.index((dx, 0))
        total = sb[j * SHARD:(j + 1) * SHARD, :].astype(F32)
        for k in (2 * dx, 2 * dx + 1):
            copy(ry.at[k], ry.at[k], y_ss.at[k], y_rs.at[k], fdev(0, 1, 0)).wait_recv()
            total = total + ry[k].astype(F32)
        return total

    xs[...] = y_sum(1).astype(BF)
    send(xs, rx, x_ss, x_rs, fdev(1, 0, 0))

    lane = lax.broadcasted_iota(jnp.int32, (1, ROWS), 1)
    for i in range(N_EP):
        part = pl.ds(i * MOST, MOST)
        four = pl.ds(i // 4 * 128, 128)
        if i:
            dev = (f, owner(i, -1))
            copy(
                cs.at[part, :], cr.at[part, :], c_ss.at[i - 1], c_rs.at[i - 1], dev
            ).wait_recv()
            copy(ps.at[:, four], pr.at[i], p_ss.at[i - 1], p_rs.at[i - 1], dev).wait_recv()
        row = jnp.concatenate([pr[i, 0:1, :].astype(F32)] * 4, axis=1)
        pv[i:i + 1, :] = jnp.where(lane // MOST == i, row, 0.0)
    for n in range(4):
        cols = slice(n * 512, n * 512 + 512)
        tok[:, cols] = dot(ptm[...], cr[:, cols]).astype(BF)
    store = pltpu.make_async_copy(tok, in_grad, l_s.at[5])
    store.start()
    picks = dot(pv[...].astype(BF), pm[...])
    got = jnp.zeros((8, TOK), F32)
    for i in range(N_EP):
        got = got + jnp.where(idt == owner(i, 1), picks[i:i + 1, :], 0.0)
    gate_grad[...] = (got / gpt).astype(BF)

    total = y_sum(0)
    copy(xs, rx, x_ss, x_rs, fdev(1, 0, 0)).wait_recv()
    total = (total + rx[...].astype(F32)).astype(BF)
    grads[...] = total
    store.wait()
    for cp in sends:
        cp.wait_send()


def hand_over(
    in_grad, gate_grad, grads, in_out, gate_out, gg, gu, gd, in_buf, gate_buf, g_buf,
    load_sems, store_sems,
):
    loads = [(in_grad.at[n * 64:n * 64 + 64, :], in_buf.at[n * 64:n * 64 + 64, :]) for n in range(4)]
    loads += [(grads.at[:, n * FF:(n + 1) * FF], g_buf.at[n]) for n in range(3)]
    loads += [(gate_grad, gate_buf)]
    stores = [(in_buf.at[n * 64:n * 64 + 64, :], in_out.at[n * 64:n * 64 + 64, :]) for n in range(4)]
    stores += [(g_buf.at[n], g) for n, g in enumerate((gg, gu, gd))]
    stores += [(gate_buf, gate_out)]
    loads = [
        pltpu.make_async_copy(src, dst, load_sems.at[n]) for n, (src, dst) in enumerate(loads)
    ]
    stores = [
        pltpu.make_async_copy(src, dst, store_sems.at[n]) for n, (src, dst) in enumerate(stores)
    ]
    for cp in loads:
        cp.start()
    for load, store in zip(loads, stores):
        load.wait()
        store.start()
    for cp in stores:
        cp.wait()


def per_device(tokens, out_grad, expert_ids, gate_probs, w_gate, w_up, w_down):
    vmem = pl.BlockSpec(memory_space=pltpu.VMEM)
    hbm = pl.BlockSpec(memory_space=pl.ANY)
    dma = pltpu.SemaphoreType.DMA
    outs = pl.pallas_call(
        kernel,
        out_shape=(
            jax.ShapeDtypeStruct((TOK, D), BF),
            jax.ShapeDtypeStruct((8, TOK), BF),
            jax.ShapeDtypeStruct((SHARD, 3 * FF), BF),
        ),
        in_specs=[hbm, hbm, vmem, vmem, hbm, hbm, hbm],
        out_specs=(hbm, vmem, vmem),
        scratch_shapes=[
            pltpu.VMEM((TOK, D), BF),
            pltpu.VMEM((TOK, D), BF),
            pltpu.VMEM((D, 3 * FF), BF),
            pltpu.VMEM((2 * FF, D), BF),
            pltpu.VMEM((ROWS, 2 * D), BF),
            pltpu.VMEM((ROWS, 2 * D), BF),
            pltpu.VMEM((D, ROWS), BF),
            pltpu.VMEM((D, ROWS), BF),
            pltpu.VMEM((ROWS, 2 * FF), BF),
            pltpu.VMEM((ROWS, FF), BF),
            pltpu.VMEM((ROWS, D), BF),
            pltpu.VMEM((ROWS, D), BF),
            pltpu.VMEM((16, ROWS), BF),
            pltpu.VMEM((N_EP, 16, 128), BF),
            pltpu.VMEM((N_EP, ROWS), F32),
            pltpu.VMEM((8, 256, 3 * FF), BF),
            pltpu.VMEM((8 * SHARD, 3 * FF), BF),
            pltpu.VMEM((4, HALF, 3 * FF), BF),
            pltpu.VMEM((4, SHARD, 3 * FF), BF),
            pltpu.VMEM((SHARD, 3 * FF), BF),
            pltpu.VMEM((SHARD, 3 * FF), BF),
            pltpu.VMEM((ROWS, TOK), BF),
            pltpu.VMEM((TOK, ROWS), BF),
            pltpu.VMEM((ROWS, 128), F32),
            dma((15,)), dma((15,)), dma((15,)), dma((15,)), dma((15,)), dma((15,)),
            dma((15,)), dma((15,)),
            dma((8,)), dma((8,)), dma((4,)), dma((4,)), dma((4,)), dma((4,)), dma, dma, dma((6,)),
        ],
        compiler_params=pltpu.CompilerParams(
            collective_id=0, has_side_effects=True, vmem_limit_bytes=62 * 2**20
        ),
        name="expert_backward",
    )(
        tokens, out_grad, expert_ids.T, gate_probs.T,
        w_gate[:, 0, :], w_up[:, 0, :], w_down[:, 0, :],
    )
    finish = pl.pallas_call(
        hand_over,
        out_shape=(
            jax.ShapeDtypeStruct((TOK, D), BF),
            jax.ShapeDtypeStruct((8, TOK), BF),
        ) + (jax.ShapeDtypeStruct((SHARD, FF), BF),) * 3,
        in_specs=[hbm] * 3,
        out_specs=(hbm,) * 5,
        scratch_shapes=[
            pltpu.VMEM((TOK, D), BF),
            pltpu.VMEM((8, TOK), BF),
            pltpu.VMEM((3, SHARD, FF), BF),
            dma((8,)), dma((8,)),
        ],
        name="hand_over",
    )
    in_grad, gate_grad, g_gate, g_up, g_down = finish(*outs)
    return in_grad, gate_grad.T, g_gate[:, None, :], g_up[:, None, :], g_down[:, None, :]


def solution(mesh):
    rows = P(("fsdp", "ep"), None)
    weight = P("fsdp", "ep", None)
    return jax.shard_map(
        per_device,
        mesh=mesh,
        in_specs=(rows,) * 4 + (weight,) * 3,
        out_specs=(rows,) * 2 + (weight,) * 3,
        check_vma=False,
    )
```
